256 devices in a mesh: ctx: 64 (over z, y_hi, x), tp: 4 (over y_lo, core).
Axes of the slice: x: 4, y: 4 (y_hi: 2, y_lo: 2; y = y_hi * 2 + y_lo), z: 8, core: 2. Of those that a mesh axis runs over, the one named last changes fastest.
Arguments:
- queries: bfloat16 [16384, 2560], P('ctx', 'tp'), may hold values from -6 to 6
- keys: bfloat16 [16384, 512], P('ctx', 'tp'), may hold values from -6 to 6
- values: bfloat16 [16384, 512], P('ctx', 'tp'), may hold values from -6 to 6
- out_weight: bfloat16 [2560, 5120], P('tp'), may hold values from -0.125 to 0.125
- cotangent: bfloat16 [16384, 5120], P('ctx', 'tp'), may hold values from -6 to 6
- doc_ids: int32 [128], replicated, may hold values from 0 to 15, never falling along the last dimension, each value on 1 to 16 neighbouring positions
Outputs:
- mixed: bfloat16 [16384, 5120], P('ctx', 'tp')
- grad_queries: bfloat16 [16384, 2560], P('ctx', 'tp')
- keys_gradient: bfloat16 [16384, 512], P('ctx', 'tp')
- values_gradient: bfloat16 [16384, 512], P('ctx', 'tp')
The draws below stay inside these ranges and needn't reach their ends.
Inputs may be any that keep to these rules, and one draw needn't show every extreme that they name: `doc_ids`: ids never fall from one block to the next; each document covers 1 to 16 blocks and one covers exactly 16.
All inputs are finite; a program needn't handle non-finite values.
Results may differ from the reference program's by a relative error of at most 0.033.
Values may be sent and summed in bfloat16 or wider, within the bound.
A program may use at most 128 MiB of HBM per device.

```python
import math
import jax
import jax.numpy as jnp
import numpy as np
from jax import lax

D = 5120
HEAD_SIZE = 128
QUERY_HEADS = 20
KEY_VALUE_HEADS = 4
BLK = 128
PACKED_TOKENS = 16384
NBLK = 128
DOC_MOST = 16
DOCS = 16


def draw_queries(key, part):
    random_seed_key = jax.random.fold_in(key, 11)
    return jnp.clip(jax.random.normal(random_seed_key, (PACKED_TOKENS, QUERY_HEADS * HEAD_SIZE), jnp.float32), -6.0, 6.0).astype(jnp.bfloat16)


def draw_keys(key, part):
    random_seed_key = jax.random.fold_in(key, 13)
    return jnp.clip(jax.random.normal(random_seed_key, (PACKED_TOKENS, KEY_VALUE_HEADS * HEAD_SIZE), jnp.float32), -6.0, 6.0).astype(jnp.bfloat16)


def steps_of(stream_key, shape, cuts, low, high):
    def one(dim, blocks):
        draws = jax.random.uniform(jax.random.fold_in(jax.random.fold_in(stream_key, 6), dim), (blocks,), jnp.float32, low / len(cuts), high / len(cuts))
        return jnp.repeat(jnp.exp(draws), shape[dim] // blocks).reshape((-1,) + (1,) * (len(shape) - dim - 1))

    gain = one(*cuts[0])
    for cut in cuts[1:]:
        gain = gain * one(*cut)
    return gain


def profile(number_of, total, most, skew):
    weights = [(1 << 20) // math.isqrt(rank ** skew) + 1 for rank in range(2, number_of + 1)]
    spare, holding = total - most - (number_of - 1), [1] * (number_of - 1)
    while spare > 0:
        movable = [i for i in range(number_of - 1) if holding[i] < most]
        whole, budget = sum([weights[i] for i in movable]), spare
        for i in movable:
            extra = min(most - holding[i], max(1, budget * weights[i] // whole), spare)
            holding[i] = holding[i] + extra
            spare = spare - extra
    return np.array([most] + holding)


def uneven_parts(stream_key, amount, total, limit, slope):
    if amount == 2:
        one = jax.random.randint(stream_key, (), max(1, total - limit), min(limit, total - 1) + 1)
        return jnp.stack([one, total - one])
    lengths = jnp.asarray(profile(amount, total, limit, slope), jnp.int32)
    pairs = (amount - 1) // 2
    donor, sink = lengths[1:1 + 2 * pairs:2], lengths[2:2 + 2 * pairs:2]
    margin = jnp.minimum(donor - 1, limit - sink)
    passed = jax.random.randint(jax.random.fold_in(stream_key, 1), (pairs,), 0, 1 << 20) % (margin + 1)
    lengths = lengths.at[1:1 + 2 * pairs:2].set(donor - passed).at[2:2 + 2 * pairs:2].set(sink + passed)
    return lengths[jax.random.permutation(jax.random.fold_in(stream_key, 2), amount)]


def normal_values(key, extent, scale, bound, pieces=(), held_as=jnp.bfloat16):
    entries = jax.random.normal(key, extent, jnp.float32) * scale
    if len(pieces) > 0:
        entries = steps_of(key, extent, pieces, -0.22, 0.18) * entries
    return jnp.clip(entries, min=-bound, max=bound).astype(held_as)


def setup_inputs(seed: int = 0) -> dict:
    splits = jax.random.split(jax.random.key(seed), 7)
    return {
        "queries": draw_queries(jax.random.fold_in(splits[6], 71), 0),
        "keys": draw_keys(jax.random.fold_in(splits[6], 71), 0),
        "values": normal_values(splits[2], (PACKED_TOKENS, KEY_VALUE_HEADS * HEAD_SIZE), 1.0, 6.0, ((0, 64), (1, 4))),
        "out_weight": normal_values(splits[3], (QUERY_HEADS * HEAD_SIZE, D), (QUERY_HEADS * HEAD_SIZE) ** -0.5, 0.125, ((0, 4),)),
        "cotangent": normal_values(splits[4], (PACKED_TOKENS, D), 1.0, 6.0, ((0, 64), (1, 4))),
        "doc_ids": jnp.searchsorted(jnp.cumsum(uneven_parts(splits[5], DOCS, NBLK, DOC_MOST, 2)), jnp.arange(NBLK), side="right").astype(jnp.int32),
    }


NEG_FILL = -1e+30

def reference(queries, keys, values, out_weight, cotangent, doc_ids):
    query_group_width = QUERY_HEADS // KEY_VALUE_HEADS
    score_scale = 1.0 / math.sqrt(HEAD_SIZE)
    query_tile_block = math.gcd(PACKED_TOKENS, 512)
    block_count = PACKED_TOKENS // query_tile_block
    window = min(PACKED_TOKENS, DOC_MOST * BLK + query_tile_block)
    key_single_precision = keys.astype(jnp.float32).reshape(PACKED_TOKENS, KEY_VALUE_HEADS, HEAD_SIZE)
    value_single_precision = values.astype(jnp.float32).reshape(PACKED_TOKENS, KEY_VALUE_HEADS, HEAD_SIZE)
    token_docs = jnp.repeat(doc_ids, BLK, total_repeat_length=PACKED_TOKENS)
    attention_gradient = jnp.dot(cotangent, out_weight.T, preferred_element_type=jnp.float32).astype(jnp.bfloat16)

    def one_block(running, block_index):
        key_sum, value_sum = running
        leading_row = block_index * query_tile_block
        key_start = jnp.clip(leading_row + query_tile_block - window, 0, PACKED_TOKENS - window).astype(jnp.int32)
        key_all = lax.dynamic_slice_in_dim(key_single_precision, key_start, window, 0)
        value_all = lax.dynamic_slice_in_dim(value_single_precision, key_start, window, 0)
        key_pos = key_start + jnp.arange(window, dtype=jnp.int32)
        key_docs = lax.dynamic_slice_in_dim(token_docs, key_start, window, 0)
        query_row_slab = lax.dynamic_slice_in_dim(queries, leading_row, query_tile_block, 0).astype(jnp.float32).reshape(query_tile_block, KEY_VALUE_HEADS, query_group_width, HEAD_SIZE)
        gradient_rows = lax.dynamic_slice_in_dim(attention_gradient, leading_row, query_tile_block, 0).astype(jnp.float32).reshape(query_tile_block, KEY_VALUE_HEADS, query_group_width, HEAD_SIZE)
        query_pos = leading_row + jnp.arange(query_tile_block, dtype=jnp.int32)
        query_docs = lax.dynamic_slice_in_dim(token_docs, leading_row, query_tile_block, 0)
        allowed = (query_docs[:, None] == key_docs[None, :]) & (key_pos[None, :] <= query_pos[:, None])
        scores = jnp.einsum('tkgd,ukd->kgtu', query_row_slab, key_all) * score_scale
        scores = jnp.where(allowed, scores, NEG_FILL)
        row_top = lax.optimization_barrier(jnp.max(scores, axis=-1, keepdims=True))
        row_total = lax.optimization_barrier(jnp.sum(jnp.where(allowed, jnp.exp(scores - row_top), 0.0), axis=-1, keepdims=True))
        lse = row_top + jnp.log(row_total)
        probs = jnp.where(allowed, jnp.exp(scores - lse), 0.0)
        weights = lax.optimization_barrier(probs.astype(jnp.bfloat16)).astype(jnp.float32)
        attn = jnp.einsum('kgtu,ukd->tkgd', weights, value_all).astype(jnp.bfloat16)
        attn_wide = lax.optimization_barrier(attn).astype(jnp.float32)
        delta = jnp.transpose(lax.optimization_barrier(jnp.sum(gradient_rows * attn_wide, axis=-1)), (1, 2, 0))
        value_add = jnp.einsum('kgtu,tkgd->ukd', weights, gradient_rows)
        prob_grad = jnp.einsum('tkgd,ukd->kgtu', gradient_rows, value_all)
        score_grad = lax.optimization_barrier((probs * (prob_grad - delta[..., None])).astype(jnp.bfloat16)).astype(jnp.float32)
        query_grad = jnp.einsum('kgtu,ukd->tkgd', score_grad, key_all) * score_scale
        key_add = jnp.einsum('kgtu,tkgd->ukd', score_grad, query_row_slab) * score_scale
        key_old = lax.dynamic_slice_in_dim(key_sum, key_start, window, 0)
        value_old = lax.dynamic_slice_in_dim(value_sum, key_start, window, 0)
        key_sum = lax.dynamic_update_slice_in_dim(key_sum, key_old + key_add, key_start, 0)
        value_sum = lax.dynamic_update_slice_in_dim(value_sum, value_old + value_add, key_start, 0)
        outputs = (attn.reshape(query_tile_block, QUERY_HEADS * HEAD_SIZE), query_grad.reshape(query_tile_block, QUERY_HEADS * HEAD_SIZE).astype(jnp.bfloat16))
        return ((key_sum, value_sum), outputs)
    initial_sums = (jnp.zeros((PACKED_TOKENS, KEY_VALUE_HEADS, HEAD_SIZE), jnp.float32), jnp.zeros((PACKED_TOKENS, KEY_VALUE_HEADS, HEAD_SIZE), jnp.float32))
    running_sums, stacked = lax.scan(one_block, initial_sums, jnp.arange(block_count, dtype=jnp.int32))
    attn_all = stacked[0].reshape(PACKED_TOKENS, QUERY_HEADS * HEAD_SIZE)
    grad_queries = stacked[1].reshape(PACKED_TOKENS, QUERY_HEADS * HEAD_SIZE)
    mixed = jnp.dot(attn_all, out_weight, preferred_element_type=jnp.float32).astype(jnp.bfloat16)
    keys_gradient = running_sums[0].reshape(PACKED_TOKENS, KEY_VALUE_HEADS * HEAD_SIZE).astype(jnp.bfloat16)
    values_gradient = running_sums[1].reshape(PACKED_TOKENS, KEY_VALUE_HEADS * HEAD_SIZE).astype(jnp.bfloat16)
    return (mixed, grad_queries, keys_gradient, values_gradient)
```

```python
import functools
import math

import jax
import jax.numpy as jnp
from jax import lax
from jax.experimental import pallas as pl
from jax.experimental.pallas import tpu as pltpu
from jax.sharding import PartitionSpec as P

HEAD = 128
BLK = 128
GROUP = 4
SLOTS = 2 * GROUP + 1
NEG = -1e30
F32 = jnp.float32
BF16 = jnp.bfloat16
MESH = pl.DeviceIdType.MESH


def dot(a, b):
    return lax.dot_general(a, b, (((1,), (0,)), ((), ())), preferred_element_type=F32)


def dot_t(a, b):
    return lax.dot_general(a, b, (((1,), (1,)), ((), ())), preferred_element_type=F32)


def kernel(
    n_ctx,
    heads,
    rows,
    chunks,
    doc,
    q_in,
    k_in,
    v_in,
    w_in,
    c_in,
    mixed,
    gq,
    gk,
    gv,
    qb,
    kv,
    wb,
    cb,
    qt,
    pb,
    mb,
    mrun,
    lrun,
    acc,
    attn_t,
    attn,
    dot_b,
    do_b,
    delta,
    dqt,
    gkv,
    g3,
    rx,
    rz,
    pp,
    pr,
    pc,
    xc,
    xr,
    po,
    q_sem,
    o_sem,
    w_sem,
    c_sem,
    ks,
    kr,
    cs,
    cr,
    gs,
    gr,
    zs,
    zr,
    ps,
    prs,
    xs,
    xrs,
):
    i = lax.axis_index("ctx")
    t = lax.axis_index("tp")
    x = lax.rem(i, GROUP)
    g0 = i - x
    partner = t + 1 - 2 * lax.rem(t, 2)
    cross = lax.rem(t + 2, 4)
    diag = lax.rem(partner + 2, 4)
    scale = 1.0 / math.sqrt(HEAD)
    c2 = scale * math.log2(math.e)

    def ctx_at(by):
        return lax.rem(i + by + n_ctx, n_ctx)

    def peer(e):
        return g0 + lax.rem(x + e + GROUP, GROUP)

    own_k = pltpu.make_async_copy(k_in, kv.at[0, 0], o_sem.at[0])
    own_v = pltpu.make_async_copy(v_in, kv.at[0, 1], o_sem.at[1])
    own_k.start()
    own_v.start()
    q_copy = pltpu.make_async_copy(q_in, qb, q_sem)
    q_copy.start()
    own_c = pltpu.make_async_copy(c_in, cb.at[t], c_sem)
    own_c.start()
    width = chunks * 256

    def w_copy(s):
        return pltpu.make_async_copy(
            w_in.at[:, pl.ds(pl.multiple_of(s * width, 256), width)], wb.at[s], w_sem.at[s]
        )

    for s in range(4):
        w_copy(s).start()

    barrier = pltpu.get_barrier_semaphore()
    for by in (4, -4, 8, -8):
        pl.semaphore_signal(barrier, inc=1, device_id=(ctx_at(by), t), device_id_type=MESH)
    for e in (1, 2, 3):
        pl.semaphore_signal(barrier, inc=1, device_id=(peer(e), t), device_id_type=MESH)
    for other in (partner, cross):
        pl.semaphore_signal(barrier, inc=1, device_id=(i, other), device_id_type=MESH)
    pl.semaphore_wait(barrier, 9)

    def send(src, dst, s_sem, r_sem, ctx, tp):
        return pltpu.make_async_remote_copy(
            src_ref=src,
            dst_ref=dst,
            send_sem=s_sem,
            recv_sem=r_sem,
            device_id=(ctx, tp),
            device_id_type=MESH,
        )

    def far(slot):
        return send(kv.at[0], kv.at[slot], ks.at[slot], kr.at[slot], ctx_at(slot), t)

    def near(src, slot, e):
        return send(kv.at[src], kv.at[slot], ks.at[slot], kr.at[slot], peer(e), t)

    def cot_send(c, to, k):
        cols = pl.ds(c * 256, 256)
        return send(c_in.at[:, cols], cb.at[t, :, cols], cs.at[k, c], cr.at[t, c], i, to)

    def cot_pass(c):
        cols = pl.ds(c * 256, 256)
        block = cb.at[cross, :, cols]
        return send(block, block, cs.at[2, c], cr.at[cross, c], i, partner)

    def cot_wait(s, c):
        cols = pl.ds(c * 256, 256)
        block = cb.at[s, :, cols]
        send(block, block, cs.at[0, c], cr.at[s, c], i, partner).wait_recv()

    own_k.wait()
    own_v.wait()
    far(4).start()
    far(8).start()
    for e in (2, 1, 3):

        @pl.when(x + e < GROUP)
        def _():
            near(0, e, e).start()

    for c in range(chunks):
        cot_send(c, cross, 0).start()
    for c in range(chunks):
        cot_send(c, partner, 1).start()

    q_copy.wait()
    for h in range(heads):
        qt[h] = qb[:, h * HEAD : (h + 1) * HEAD].T

    lane = lax.broadcasted_iota(jnp.int32, (1, rows), 1)
    q_doc = jnp.where(lane < BLK, doc[2 * i], doc[2 * i + 1])

    def first_slot():
        k_blk = kv[0, 0]
        v_t = kv[0, 1].T
        key = lax.broadcasted_iota(jnp.int32, (rows, rows), 0)
        query = lax.broadcasted_iota(jnp.int32, (rows, rows), 1)
        k_doc = jnp.where(key < BLK, doc[2 * i], doc[2 * i + 1])
        allowed = (key <= query) & (k_doc == q_doc)
        for h in range(heads):
            s = jnp.where(allowed, dot(k_blk, qt[h]) * c2, NEG)
            m = jnp.max(s, axis=0, keepdims=True)
            p = jnp.exp2(s - m)
            lrun[h] = jnp.sum(p, axis=0, keepdims=True)
            p = p.astype(BF16)
            pb[0, h] = p
            mrun[h] = m
            mb[0, h] = m
            acc[h] = dot(v_t, p)

    def fwd_slot(d):
        src = ctx_at(-d)
        k_blk = kv[d, 0]
        v_t = kv[d, 1].T
        b0 = jnp.where(q_doc == doc[2 * src], 0.0, NEG)
        b1 = jnp.where(q_doc == doc[2 * src + 1], 0.0, NEG)
        for h in range(heads):
            s = dot(k_blk, qt[h]) * c2
            s0, s1 = s[:BLK], s[BLK:]
            m_old = mrun[h]
            m = jnp.maximum(
                m_old,
                jnp.maximum(
                    jnp.max(s0, axis=0, keepdims=True) + b0,
                    jnp.max(s1, axis=0, keepdims=True) + b1,
                ),
            )
            alpha = jnp.exp2(m_old - m)
            p0 = jnp.exp2(s0 - (m - b0))
            p1 = jnp.exp2(s1 - (m - b1))
            lrun[h] = (
                lrun[h] * alpha
                + jnp.sum(p0, axis=0, keepdims=True)
                + jnp.sum(p1, axis=0, keepdims=True)
            )
            p = jnp.concatenate([p0, p1], axis=0).astype(BF16)
            pb[d, h] = p
            mrun[h] = m
            mb[d, h] = m
            acc[h] = acc[h] * alpha + dot(v_t, p)

    first_slot()
    far(4).wait_recv()
    for e in (2, 1, 3):

        @pl.when(x + e < GROUP)
        def _():
            near(4, e + 4, e).start()

        @pl.when(x + e >= GROUP)
        def _():
            near(4, e, e).start()

    far(8).wait_recv()
    for e in (2, 1, 3):

        @pl.when(x + e >= GROUP)
        def _():
            near(8, e + 4, e).start()

    def fwd_step(k, carry):
        d = jnp.where(k < 2, 4 * (k + 1), jnp.where(k < 5, k - 1, k))
        d = jnp.where(k == 3, 3, jnp.where(k == 4, 2, jnp.where(k == 6, 7, jnp.where(k == 7, 6, d))))

        @pl.when(k >= 2)
        def _():
            near(0, d, 1).wait_recv()

        fwd_slot(d)
        return carry

    lax.fori_loop(0, SLOTS - 1, fwd_step, 0)

    for h in range(heads):
        a = (acc[h] / lrun[h]).astype(BF16)
        attn_t[h] = a
        attn[:, h * HEAD : (h + 1) * HEAD] = a.T

    def part(s, c):
        cols = pl.ds(pl.multiple_of(c * 256, 256), 256)
        return dot(attn[...], wb[s, :, cols])

    def to_partner(k, c):
        return send(pp.at[k, c], pr.at[k, c], ps.at[k, c], prs.at[k, c], i, partner)

    def to_cross(c):
        return send(xc.at[c], xr.at[c], xs.at[c], xrs.at[c], i, cross)

    for s in range(4):
        w_copy(s).wait()

    def diag_step(c, carry):
        pp[0, c] = part(diag, c).astype(BF16)
        to_partner(0, c).start()
        return carry

    lax.fori_loop(0, chunks, diag_step, 0)

    def cross_step(c, carry):
        mine = part(cross, c)
        to_partner(0, c).wait_recv()
        xc[c] = (mine + pr[0, c].astype(F32)).astype(BF16)
        to_cross(c).start()
        return carry

    lax.fori_loop(0, chunks, cross_step, 0)

    def partner_step(c, carry):
        pp[1, c] = part(partner, c).astype(BF16)
        to_partner(1, c).start()
        po[c] = part(t, c)
        return carry

    lax.fori_loop(0, chunks, partner_step, 0)

    for c in range(chunks):
        cot_wait(cross, c)
        cot_pass(c).start()
    own_c.wait()
    grad = dot_t(wb[t], cb[t])
    for c in range(chunks):
        cot_wait(partner, c)
    grad = grad + dot_t(wb[partner], cb[partner])
    grad = grad + dot_t(wb[cross], cb[cross])
    for c in range(chunks):
        cot_wait(diag, c)
    grad = grad + dot_t(wb[diag], cb[diag])
    for h in range(heads):
        do_t = grad[h * HEAD : (h + 1) * HEAD].astype(BF16)
        dot_b[h] = do_t
        do_b[h] = do_t.T
        delta[h] = jnp.sum(do_t.astype(F32) * attn_t[h].astype(F32), axis=0, keepdims=True)
        dqt[h] = jnp.zeros((HEAD, rows), F32)
        lrun[h] = 1.0 / lrun[h]

    def bwd_slot(d):
        k_t = kv[d, 0].T
        v_blk = kv[d, 1]
        dk = jnp.zeros((rows, HEAD), F32)
        dv = jnp.zeros((rows, HEAD), F32)
        for h in range(heads):
            f = jnp.exp2(mb[d, h] - mrun[h]) * lrun[h]
            p = pb[d, h].astype(F32) * f
            dv = dv + dot(p.astype(BF16), do_b[h])
            ds = (p * (dot(v_blk, dot_b[h]) - delta[h])).astype(BF16)
            dk = dk + dot(ds, qb[:, h * HEAD : (h + 1) * HEAD])
            dqt[h] = dqt[h] + dot(k_t, ds)
        return dk * scale, dv

    def grad_near(e, j):
        return send(
            gkv.at[e + 4 * j], rx.at[e - 1, j], gs.at[e - 1, j], gr.at[e - 1, j], peer(-e), t
        )

    def bwd_step(k, carry):
        e = jnp.where(k < 2, 2, jnp.where(k < 4, 1, 3))
        j = lax.rem(k, 2)
        d = e + 4 * j
        dk, dv = bwd_slot(d)
        gkv[d, 0] = dk.astype(BF16)
        gkv[d, 1] = dv.astype(BF16)
        grad_near(e, j).start()
        return carry

    lax.fori_loop(0, 6, bwd_step, 0)

    def bwd_own(k, carry):
        dk, dv = bwd_slot(8 - 4 * k)
        g3[2 - k, 0] = dk
        g3[2 - k, 1] = dv
        return carry

    lax.fori_loop(0, 3, bwd_own, 0)

    for e in (2, 1, 3):
        base = lax.div(x + e, GROUP)
        for j in range(2):
            grad_near(e, j).wait_recv()
            g3[base + j] = g3[base + j] + rx[e - 1, j].astype(F32)

    def grad_far(k):
        return send(gkv.at[4 * k + 4], rz.at[k], zs.at[k], zr.at[k], ctx_at(-4 * k - 4), t)

    for k in range(2):
        gkv[4 * k + 4] = g3[k + 1].astype(BF16)
        grad_far(k).start()

    for h in range(heads):
        gq[:, h * HEAD : (h + 1) * HEAD] = (dqt[h].T * scale).astype(BF16)
    for c in range(chunks):
        to_partner(1, c).wait_recv()
        to_cross(c).wait_recv()
        mixed[:, c * 256 : (c + 1) * 256] = (
            po[c] + pr[1, c].astype(F32) + xr[c].astype(F32)
        ).astype(BF16)
    for k in range(2):
        grad_far(k).wait_recv()
    total = g3[0] + rz[0].astype(F32) + rz[1].astype(F32)
    gk[...] = total[0].astype(BF16)
    gv[...] = total[1].astype(BF16)

    for slot in (4, 8):
        far(slot).wait_send()
    for e in (1, 2, 3):
        near(0, e, e).wait_send()
        near(0, e + 4, e).wait_send()
        for j in range(2):
            grad_near(e, j).wait_send()
    for k in range(2):
        grad_far(k).wait_send()
    for c in range(chunks):
        cot_send(c, cross, 0).wait_send()
        cot_send(c, partner, 1).wait_send()
        cot_pass(c).wait_send()
        to_partner(0, c).wait_send()
        to_partner(1, c).wait_send()
        to_cross(c).wait_send()


def on_device(queries, keys, values, out_weight, cotangent, doc_ids):
    n_ctx = lax.axis_size("ctx")
    rows = queries.shape[0]
    heads = queries.shape[1] // HEAD
    chunks = cotangent.shape[1] // 256
    any_space = pl.BlockSpec(memory_space=pl.ANY)
    vmem = pl.BlockSpec(memory_space=pltpu.VMEM)
    dma = pltpu.SemaphoreType.DMA
    return pl.pallas_call(
        functools.partial(kernel, n_ctx, heads, rows, chunks),
        out_shape=(
            jax.ShapeDtypeStruct(cotangent.shape, BF16),
            jax.ShapeDtypeStruct(queries.shape, BF16),
            jax.ShapeDtypeStruct(keys.shape, BF16),
            jax.ShapeDtypeStruct(values.shape, BF16),
        ),
        in_specs=[pl.BlockSpec(memory_space=pltpu.SMEM)] + [any_space] * 5,
        out_specs=(vmem,) * 4,
        scratch_shapes=[
            pltpu.VMEM((rows, heads * HEAD), BF16),
            pltpu.VMEM((SLOTS, 2, rows, HEAD), BF16),
            pltpu.VMEM((4, heads * HEAD, chunks * 256), BF16),
            pltpu.VMEM((4, rows, chunks * 256), BF16),
            pltpu.VMEM((heads, HEAD, rows), BF16),
            pltpu.VMEM((SLOTS, heads, rows, rows), BF16),
            pltpu.VMEM((SLOTS, heads, 1, rows), F32),
            pltpu.VMEM((heads, 1, rows), F32),
            pltpu.VMEM((heads, 1, rows), F32),
            pltpu.VMEM((heads, HEAD, rows), F32),
            pltpu.VMEM((heads, HEAD, rows), BF16),
            pltpu.VMEM((rows, heads * HEAD), BF16),
            pltpu.VMEM((heads, HEAD, rows), BF16),
            pltpu.VMEM((heads, rows, HEAD), BF16),
            pltpu.VMEM((heads, 1, rows), F32),
            pltpu.VMEM((heads, HEAD, rows), F32),
            pltpu.VMEM((SLOTS, 2, rows, HEAD), BF16),
            pltpu.VMEM((3, 2, rows, HEAD), F32),
            pltpu.VMEM((3, 2, 2, rows, HEAD), BF16),
            pltpu.VMEM((2, 2, rows, HEAD), BF16),
            pltpu.VMEM((2, chunks, rows, 256), BF16),
            pltpu.VMEM((2, chunks, rows, 256), BF16),
            pltpu.VMEM((1, 8, 128), F32),
            pltpu.VMEM((chunks, rows, 256), BF16),
            pltpu.VMEM((chunks, rows, 256), BF16),
            pltpu.VMEM((chunks, rows, 256), F32),
            dma,
            dma((2,)),
            dma((4,)),
            dma,
            dma((SLOTS,)),
            dma((SLOTS,)),
            dma((3, chunks)),
            dma((4, chunks)),
            dma((3, 2)),
            dma((3, 2)),
            dma((2,)),
            dma((2,)),
            dma((2, chunks)),
            dma((2, chunks)),
            dma((chunks,)),
            dma((chunks,)),
        ],
        compiler_params=pltpu.CompilerParams(
            collective_id=0, has_side_effects=True, vmem_limit_bytes=60 * 1024 * 1024
        ),
    )(doc_ids, queries, keys, values, out_weight, cotangent)


def solution(mesh):
    return jax.shard_map(
        on_device,
        mesh=mesh,
        in_specs=(
            P("ctx", "tp"),
            P("ctx", "tp"),
            P("ctx", "tp"),
            P("tp", None),
            P("ctx", "tp"),
            P(),
        ),
        out_specs=(P("ctx", "tp"), P("ctx", "tp"), P("ctx", "tp"), P("ctx", "tp")),
        check_vma=False,
    )
```

```python
import contextlib
import functools
import math

import jax
import jax.numpy as jnp
from jax import lax
from jax.experimental import pallas as pl
from jax.experimental.pallas import tpu as pltpu
from jax.sharding import PartitionSpec as P

HEAD = 128
BLK = 128
GROUP = 4
SLOTS = 2 * GROUP + 1
NEG = -1e30
F32 = jnp.float32
BF16 = jnp.bfloat16
MESH = pl.DeviceIdType.MESH


def dot(a, b):
    return lax.dot_general(a, b, (((1,), (0,)), ((), ())), preferred_element_type=F32)


def dot_t(a, b):
    return lax.dot_general(a, b, (((1,), (1,)), ((), ())), preferred_element_type=F32)


def scope(name):
    return contextlib.nullcontext()


def kernel(
    n_ctx,
    heads,
    rows,
    chunks,
    doc_in,
    q_in,
    k_in,
    v_in,
    w_in,
    c_in,
    mixed,
    gq,
    gk,
    gv,
    doc,
    qb,
    qs,
    kv,
    wb,
    cb,
    qt,
    sb,
    pb,
    mg,
    m8,
    mrun,
    l8,
    linv,
    acc,
    attn_t,
    attn,
    gt,
    dot_b,
    do_b,
    delta,
    ktb,
    gkv,
    g3,
    relay,
    rx,
    rz,
    pp,
    pr,
    xc,
    xr,
    po,
    d_sem,
    q_sem,
    o_sem,
    w_sem,
    c_sem,
    ks,
    kr,
    cs,
    cr,
    rs,
    rr,
    gs,
    gr,
    zs,
    zr,
    ps,
    prs,
    xs,
    xrs,
):
    i = lax.axis_index("ctx")
    t = lax.axis_index("tp")
    x = lax.rem(i, GROUP)
    g0 = i - x
    partner = t + 1 - 2 * lax.rem(t, 2)
    cross = lax.rem(t + 2, 4)
    diag = lax.rem(partner + 2, 4)
    scale = 1.0 / math.sqrt(HEAD)
    c2 = scale * math.log2(math.e)
    last = lax.div(x, GROUP - 1)
    first = lax.div(GROUP - 1 - x, GROUP - 1)

    def ctx_at(by):
        return lax.rem(i + by + n_ctx, n_ctx)

    def peer(e):
        return g0 + lax.rem(x + e + GROUP, GROUP)

    own_k = pltpu.make_async_copy(k_in, kv.at[0, 0], o_sem.at[0])
    own_v = pltpu.make_async_copy(v_in, kv.at[0, 1], o_sem.at[1])
    own_k.start()
    own_v.start()
    doc_copy = pltpu.make_async_copy(doc_in, doc, d_sem)
    doc_copy.start()
    q_copy = pltpu.make_async_copy(q_in, qb, q_sem)
    q_copy.start()
    own_c = pltpu.make_async_copy(c_in, cb.at[t], c_sem)
    own_c.start()
    width = chunks * 256

    def w_copy(s):
        return pltpu.make_async_copy(
            w_in.at[:, pl.ds(pl.multiple_of(s * width, 256), width)], wb.at[s], w_sem.at[s]
        )

    for s in (t, partner, diag, cross):
        w_copy(s).start()

    barrier = pltpu.get_barrier_semaphore()
    for by in (4, -4, 8, -8):
        pl.semaphore_signal(barrier, inc=1, device_id=(ctx_at(by), t), device_id_type=MESH)
    for e in (1, 3):
        pl.semaphore_signal(barrier, inc=1, device_id=(peer(e), t), device_id_type=MESH)
    for other in (partner, cross):
        pl.semaphore_signal(barrier, inc=1, device_id=(i, other), device_id_type=MESH)
    with scope("barrier"):
        pl.semaphore_wait(barrier, 8)

    def send(src, dst, s_sem, r_sem, ctx, tp):
        return pltpu.make_async_remote_copy(
            src_ref=src,
            dst_ref=dst,
            send_sem=s_sem,
            recv_sem=r_sem,
            device_id=(ctx, tp),
            device_id_type=MESH,
        )

    def far(place):
        return send(kv.at[0], kv.at[place], ks.at[place], kr.at[place], ctx_at(4 * place), t)

    def near(src, place, e):
        return send(kv.at[src], kv.at[place], ks.at[place], kr.at[place], peer(e), t)

    def arrived(place):
        near(0, place, 1).wait_recv()

    def cot_send(c, to, k):
        cols = pl.ds(c * 256, 256)
        return send(c_in.at[:, cols], cb.at[t, :, cols], cs.at[k, c], cr.at[t, c], i, to)

    def cot_pass(c):
        cols = pl.ds(c * 256, 256)
        block = cb.at[cross, :, cols]
        return send(block, block, cs.at[2, c], cr.at[cross, c], i, partner)

    def cot_wait(s, c):
        cols = pl.ds(c * 256, 256)
        block = cb.at[s, :, cols]
        send(block, block, cs.at[0, c], cr.at[s, c], i, partner).wait_recv()

    own_k.wait()
    own_v.wait()
    far(1).start()
    far(2).start()
    for e in (1, 3):

        @pl.when(x + e < GROUP)
        def _():
            near(0, 2 + e, e).start()

    for c in range(chunks):
        cot_send(c, partner, 1).start()

    q_copy.wait()
    doc_copy.wait()
    for h in range(heads):
        q_head = qb[:, h * HEAD : (h + 1) * HEAD]
        qs[h] = q_head
        qt[h] = q_head.T

    lane = lax.broadcasted_iota(jnp.int32, (1, rows), 1)
    q_doc = jnp.where(lane < BLK, doc[2 * i], doc[2 * i + 1])

    def bias(d):
        src = ctx_at(-d)
        return [jnp.where(q_doc == doc[2 * src + b], 0.0, NEG) for b in range(2)]

    def scores(k, place, d):
        k_blk = kv[place, 0]
        if d is None:
            key = lax.broadcasted_iota(jnp.int32, (rows, rows), 0)
            query = lax.broadcasted_iota(jnp.int32, (rows, rows), 1)
            k_doc = jnp.where(key < BLK, doc[2 * i], doc[2 * i + 1])
            allowed = (key <= query) & (k_doc == q_doc)
        else:
            b0, b1 = bias(d)
        for h in range(heads):
            s = dot(k_blk, qt[h])
            if d is None:
                s = jnp.where(allowed, s, NEG)
            sb[k, h] = s
            top = jnp.max(s.reshape(2, BLK // 8, 8, rows), axis=1) * c2
            if d is None:
                top = jnp.maximum(top[0], top[1])
            else:
                top = jnp.maximum(top[0] + b0, top[1] + b1)
            m8[h] = top if k == 0 else jnp.maximum(m8[h], top)

    def weigh(group, entries):
        tops = []
        alphas = []
        for h in range(heads):
            m = jnp.max(m8[h], axis=0, keepdims=True)
            if group > 0:
                m = jnp.maximum(m, mrun[h])
                alphas.append(jnp.exp2(mrun[h] - m))
            mrun[h] = m
            mg[group, h] = m
            tops.append(m)
        v_t = jnp.concatenate([kv[place, 1].T for place, _ in entries], axis=1)
        shifts = [None if d is None else bias(d) for _, d in entries]
        for h in range(heads):
            blocks = []
            total = None
            for k, (place, d) in enumerate(entries):
                s = sb[k, h] * c2
                if d is None:
                    p = jnp.exp2(s - tops[h])
                else:
                    b0, b1 = shifts[k]
                    p = jnp.concatenate(
                        [jnp.exp2(s[:BLK] - (tops[h] - b0)), jnp.exp2(s[BLK:] - (tops[h] - b1))],
                        axis=0,
                    )
                part_sum = jnp.sum(p.reshape(rows // 8, 8, rows), axis=0)
                total = part_sum if total is None else total + part_sum
                p = p.astype(BF16)
                pb[place, h] = p
                blocks.append(p)
            out = dot(v_t, jnp.concatenate(blocks, axis=0))
            if group > 0:
                total = total + l8[h] * alphas[h]
                out = out + acc[h] * alphas[h]
            l8[h] = total
            acc[h] = out

    with scope("slot0"):
        scores(0, 0, None)
    for c in range(chunks):
        cot_send(c, cross, 0).start()
    with scope("grad0"):
        w_copy(t).wait()
        own_c.wait()
        gt[...] = dot_t(wb[t], cb[t])
    with scope("wait4"):
        far(1).wait_recv()
    for e in (1, 3):

        @pl.when(x + e < GROUP)
        def _():
            near(1, 3 + e, e).start()

        @pl.when(x + e >= GROUP)
        def _():
            near(1, 2 + e, e).start()

    with scope("wait8"):
        far(2).wait_recv()
    for e in (1, 3):

        @pl.when(x + e >= GROUP)
        def _():
            near(2, 3 + e, e).start()

    with scope("groupA"):
        scores(1, 1, 4)
        scores(2, 2, 8)
        weigh(0, [(0, None), (1, 4), (2, 8)])

    up, down = 3 + last, 6 - first
    with scope("waitup"):
        arrived(up)
    near(up, 7, 1).start()
    with scope("waitdown"):
        arrived(down)
    near(down, 8, -1).start()
    with scope("grad1"):
        w_copy(partner).wait()
        for c in range(chunks):
            cot_wait(partner, c)
        gt[...] += dot_t(wb[partner], cb[partner])
    rest_up, rest_down = 4 - last, 5 + first
    group_b = [
        (up, 1 + 4 * last),
        (down, 7 - 4 * first),
        (rest_up, 5 - 4 * last),
        (rest_down, 3 + 4 * first),
    ]
    for k, (place, d) in enumerate(group_b):
        if k >= 2:
            with scope("waitb"):
                arrived(place)
        with scope("scoreb"):
            scores(k, place, d)
    with scope("groupB"):
        weigh(1, group_b)
    group_c = [(7, 2), (8, 6)]
    for k, (place, d) in enumerate(group_c):
        with scope("waitc"):
            arrived(place)
        scores(k, place, d)
    with scope("groupC"):
        weigh(2, group_c)

        for h in range(heads):
            inv = 1.0 / jnp.sum(l8[h], axis=0, keepdims=True)
            linv[h] = inv
            a = (acc[h] * inv).astype(BF16)
            attn_t[h] = a
            attn[:, h * HEAD : (h + 1) * HEAD] = a.T

    def part(s, c):
        return dot(attn[...], wb[s, :, c * 256 : (c + 1) * 256])

    def to_partner(k, c):
        return send(pp.at[k, c], pr.at[k, c], ps.at[k, c], prs.at[k, c], i, partner)

    def to_cross(c):
        return send(xc.at[c], xr.at[c], xs.at[c], xrs.at[c], i, cross)

    with scope("diag"):
        w_copy(diag).wait()
        for c in range(chunks):
            pp[0, c] = part(diag, c).astype(BF16)
            to_partner(0, c).start()
    with scope("cross"):
        w_copy(cross).wait()
        for c in range(chunks):
            po[c] = part(cross, c)
    with scope("rs1"):
        for c in range(chunks):
            to_partner(0, c).wait_recv()
            xc[c] = (po[c] + pr[0, c].astype(F32)).astype(BF16)
            to_cross(c).start()

    with scope("cotx"):
        for c in range(chunks):
            cot_wait(cross, c)
            cot_pass(c).start()
    with scope("grad2"):
        gt[...] += dot_t(wb[cross], cb[cross])
    with scope("cotd"):
        for c in range(chunks):
            cot_wait(diag, c)
    with scope("grad3"):
        gt[...] += dot_t(wb[diag], cb[diag])
        for h in range(heads):
            do_t = gt[h * HEAD : (h + 1) * HEAD].astype(BF16)
            dot_b[h] = do_t
            do_b[h] = do_t.T
            delta[h] = jnp.sum(do_t.astype(F32) * attn_t[h].astype(F32), axis=0, keepdims=True)

    def bwd_group(places, group):
        weights = [[] for _ in places]
        grads = [[] for _ in places]
        for h in range(heads):
            f = jnp.exp2(mg[group, h] - mrun[h]) * linv[h]
            for n, place in enumerate(places):
                p = pb[place, h].astype(F32) * f
                weights[n].append(p.astype(BF16))
                ds = (p * (dot(kv[place, 1], dot_b[h]) - delta[h])).astype(BF16)
                pb[place, h] = ds
                grads[n].append(ds)
        out = []
        for n in range(len(places)):
            dv = dot(jnp.concatenate(weights[n], axis=1), do_b[...].reshape(heads * rows, HEAD))
            dk = dot(jnp.concatenate(grads[n], axis=1), qs[...].reshape(heads * rows, HEAD))
            out.append((dk * scale, dv))
        return out

    def grad_relay(side):
        return send(
            gkv.at[7 + side], relay.at[side], rs.at[side], rr.at[side], peer(2 * side - 1), t
        )

    def grad_near(side, j):
        return send(
            gkv.at[3 + 2 * side + j],
            rx.at[side, j],
            gs.at[side, j],
            gr.at[side, j],
            peer(2 * side - 1),
            t,
        )

    def bwd_step(k, carry):
        j_up = jnp.where(k == 1, 1 - last, last)
        j_down = jnp.where(k == 1, first, 1 - first)
        places = [jnp.where(k == 0, 7, 3 + j_up), jnp.where(k == 0, 8, 5 + j_down)]
        with scope("bwd"):
            outs = bwd_group(places, jnp.where(k == 0, 2, 1))

        @pl.when(k < 2)
        def _():
            for place, (dk, dv) in zip(places, outs):
                gkv[place, 0] = dk.astype(BF16)
                gkv[place, 1] = dv.astype(BF16)

        @pl.when(k == 2)
        def _():
            for side, (place, (dk, dv)) in enumerate(zip(places, outs)):
                with scope("waitrelay"):
                    grad_relay(side).wait_recv()
                gkv[place, 0] = (dk + relay[side, 0].astype(F32)).astype(BF16)
                gkv[place, 1] = (dv + relay[side, 1].astype(F32)).astype(BF16)

        @pl.when(k == 0)
        def _():
            grad_relay(0).start()
            grad_relay(1).start()

        @pl.when(k > 0)
        def _():
            grad_near(0, j_up).start()
            grad_near(1, j_down).start()

        return carry

    lax.fori_loop(0, 3, bwd_step, 0)

    with scope("bwdown"):
        for n, (dk, dv) in enumerate(bwd_group([0, 1, 2], 0)):
            g3[n, 0] = dk
            g3[n, 1] = dv

    with scope("partner"):
        for c in range(chunks):
            pp[1, c] = part(partner, c).astype(BF16)
            to_partner(1, c).start()
        for c in range(chunks):
            po[c] = part(t, c)

    for side, e in enumerate((1, 3)):
        base = lax.div(x + e, GROUP)
        for j in range(2):
            with scope("gradnear"):
                grad_near(side, j).wait_recv()
            g3[base + j] = g3[base + j] + rx[side, j].astype(F32)

    def grad_far(k):
        return send(gkv.at[k + 1], rz.at[k], zs.at[k], zr.at[k], ctx_at(-4 * k - 4), t)

    for k in range(2):
        gkv[k + 1] = g3[k + 1].astype(BF16)
        grad_far(k).start()

    with scope("dq"):
        for n in range(SLOTS):
            ktb[:, n * rows : (n + 1) * rows] = kv[n, 0].T
        for h in range(heads):
            dq_t = dot(ktb[...], pb[:, h].reshape(SLOTS * rows, rows))
            gq[:, h * HEAD : (h + 1) * HEAD] = (dq_t * scale).T.astype(BF16)
    for c in range(chunks):
        with scope("rscross"):
            to_partner(1, c).wait_recv()
            to_cross(c).wait_recv()
        mixed[:, c * 256 : (c + 1) * 256] = (
            po[c] + pr[1, c].astype(F32) + xr[c].astype(F32)
        ).astype(BF16)
    for k in range(2):
        with scope("gradfar"):
            grad_far(k).wait_recv()
    total = g3[0] + rz[0].astype(F32) + rz[1].astype(F32)
    gk[...] = total[0].astype(BF16)
    gv[...] = total[1].astype(BF16)

    for place in range(1, SLOTS):
        near(0, place, 1).wait_send()
    for side in range(2):
        grad_relay(side).wait_send()
        for j in range(2):
            grad_near(side, j).wait_send()
    for k in range(2):
        grad_far(k).wait_send()
    for c in range(chunks):
        cot_send(c, cross, 0).wait_send()
        cot_send(c, partner, 1).wait_send()
        cot_pass(c).wait_send()
        to_partner(0, c).wait_send()
        to_partner(1, c).wait_send()
        to_cross(c).wait_send()


def leave(*refs):
    count = (len(refs) - 1) // 2
    sem = refs[-1]
    copies = [
        pltpu.make_async_copy(refs[n], refs[count + n], sem.at[n]) for n in range(count)
    ]
    for copy in copies:
        copy.start()
    for copy in copies:
        copy.wait()


def on_device(queries, keys, values, out_weight, cotangent, doc_ids):
    n_ctx = lax.axis_size("ctx")
    rows = queries.shape[0]
    heads = queries.shape[1] // HEAD
    chunks = cotangent.shape[1] // 256
    any_space = pl.BlockSpec(memory_space=pl.ANY)
    hbm = pl.BlockSpec(memory_space=pltpu.HBM)
    vmem = pl.BlockSpec(memory_space=pltpu.VMEM)
    dma = pltpu.SemaphoreType.DMA
    shapes = tuple(
        jax.ShapeDtypeStruct(like.shape, BF16) for like in (cotangent, queries, keys, values)
    )
    results = pl.pallas_call(
        functools.partial(kernel, n_ctx, heads, rows, chunks),
        out_shape=shapes,
        in_specs=[hbm] * 6,
        out_specs=(vmem,) * 4,
        scratch_shapes=[
            pltpu.SMEM(doc_ids.shape, jnp.int32),
            pltpu.VMEM((rows, heads * HEAD), BF16),
            pltpu.VMEM((heads, rows, HEAD), BF16),
            pltpu.VMEM((SLOTS, 2, rows, HEAD), BF16),
            pltpu.VMEM((4, heads * HEAD, chunks * 256), BF16),
            pltpu.VMEM((4, rows, chunks * 256), BF16),
            pltpu.VMEM((heads, HEAD, rows), BF16),
            pltpu.VMEM((4, heads, rows, rows), F32),
            pltpu.VMEM((SLOTS, heads, rows, rows), BF16),
            pltpu.VMEM((3, heads, 1, rows), F32),
            pltpu.VMEM((heads, 8, rows), F32),
            pltpu.VMEM((heads, 1, rows), F32),
            pltpu.VMEM((heads, 8, rows), F32),
            pltpu.VMEM((heads, 1, rows), F32),
            pltpu.VMEM((heads, HEAD, rows), F32),
            pltpu.VMEM((heads, HEAD, rows), BF16),
            pltpu.VMEM((rows, heads * HEAD), BF16),
            pltpu.VMEM((heads * HEAD, rows), F32),
            pltpu.VMEM((heads, HEAD, rows), BF16),
            pltpu.VMEM((heads, rows, HEAD), BF16),
            pltpu.VMEM((heads, 1, rows), F32),
            pltpu.VMEM((HEAD, SLOTS * rows), BF16),
            pltpu.VMEM((SLOTS, 2, rows, HEAD), BF16),
            pltpu.VMEM((3, 2, rows, HEAD), F32),
            pltpu.VMEM((2, 2, rows, HEAD), BF16),
            pltpu.VMEM((2, 2, 2, rows, HEAD), BF16),
            pltpu.VMEM((2, 2, rows, HEAD), BF16),
            pltpu.VMEM((2, chunks, rows, 256), BF16),
            pltpu.VMEM((2, chunks, rows, 256), BF16),
            pltpu.VMEM((chunks, rows, 256), BF16),
            pltpu.VMEM((chunks, rows, 256), BF16),
            pltpu.VMEM((chunks, rows, 256), F32),
            dma,
            dma,
            dma((2,)),
            dma((4,)),
            dma,
            dma((SLOTS,)),
            dma((SLOTS,)),
            dma((3, chunks)),
            dma((4, chunks)),
            dma((2,)),
            dma((2,)),
            dma((2, 2)),
            dma((2, 2)),
            dma((2,)),
            dma((2,)),
            dma((2, chunks)),
            dma((2, chunks)),
            dma((chunks,)),
            dma((chunks,)),
        ],
        compiler_params=pltpu.CompilerParams(
            collective_id=0, has_side_effects=True, vmem_limit_bytes=50 * 1024 * 1024
        ),
    )(
        *[
            pltpu.with_memory_space_constraint(a, pltpu.HBM)
            for a in (doc_ids, queries, keys, values, out_weight, cotangent)
        ]
    )
    return pl.pallas_call(
        leave,
        out_shape=shapes,
        in_specs=[any_space] * 4,
        out_specs=(any_space,) * 4,
        scratch_shapes=[dma((4,))],
        compiler_params=pltpu.CompilerParams(vmem_limit_bytes=1024 * 1024),
    )(*results)


def solution(mesh):
    return jax.shard_map(
        on_device,
        mesh=mesh,
        in_specs=(
            P("ctx", "tp"),
            P("ctx", "tp"),
            P("ctx", "tp"),
            P("tp", None),
            P("ctx", "tp"),
            P(),
        ),
        out_specs=(P("ctx", "tp"), P("ctx", "tp"), P("ctx", "tp"), P("ctx", "tp")),
        check_vma=False,
    )
```

```python
import contextlib
import functools
import math

import jax
import jax.numpy as jnp
from jax import lax
from jax.experimental import pallas as pl
from jax.experimental.pallas import tpu as pltpu
from jax.sharding import PartitionSpec as P

HEAD = 128
BLK = 128
GROUP = 4
SLOTS = 2 * GROUP + 1
NEG = -1e30
F32 = jnp.float32
BF16 = jnp.bfloat16
MESH = pl.DeviceIdType.MESH


def dot(a, b):
    return lax.dot_general(a, b, (((1,), (0,)), ((), ())), preferred_element_type=F32)


def dot_t(a, b):
    return lax.dot_general(a, b, (((1,), (1,)), ((), ())), preferred_element_type=F32)


def scope(name):
    return contextlib.nullcontext()


def kernel(
    n_ctx,
    heads,
    rows,
    chunks,
    doc_in,
    q_in,
    k_in,
    v_in,
    w_in,
    c_in,
    mixed_out,
    gq_out,
    gk_out,
    gv_out,
    mixed,
    gq,
    gk,
    gv,
    out_sem,
    doc,
    qb,
    qs,
    kv,
    wb,
    cb,
    qt,
    sb,
    pb,
    mg,
    m8,
    mrun,
    l8,
    linv,
    acc,
    attn_t,
    attn,
    gt,
    dot_b,
    do_b,
    delta,
    ktb,
    gkv,
    g3,
    relay,
    rx,
    rz,
    pp,
    pr,
    xc,
    xr,
    po,
    d_sem,
    q_sem,
    o_sem,
    w_sem,
    c_sem,
    ks,
    kr,
    cs,
    cr,
    rr,
    gs,
    gr,
    zr,
    ps,
    prs,
    xs,
    xrs,
):
    i = lax.axis_index("ctx")
    t = lax.axis_index("tp")
    x = lax.rem(i, GROUP)
    g0 = i - x
    partner = t + 1 - 2 * lax.rem(t, 2)
    cross = lax.rem(t + 2, 4)
    diag = lax.rem(partner + 2, 4)
    scale = 1.0 / math.sqrt(HEAD)
    c2 = scale * math.log2(math.e)
    last = lax.div(x, GROUP - 1)
    first = lax.div(GROUP - 1 - x, GROUP - 1)

    def ctx_at(by):
        return lax.rem(i + by + n_ctx, n_ctx)

    def peer(e):
        return g0 + lax.rem(x + e + GROUP, GROUP)

    barrier = pltpu.get_barrier_semaphore()
    for by in (4, -4, 8, -8):
        pl.semaphore_signal(barrier, inc=1, device_id=(ctx_at(by), t), device_id_type=MESH)
    for e in (1, 3):
        pl.semaphore_signal(barrier, inc=1, device_id=(peer(e), t), device_id_type=MESH)
    for other in (partner, cross):
        pl.semaphore_signal(barrier, inc=1, device_id=(i, other), device_id_type=MESH)

    own_k = pltpu.make_async_copy(k_in, kv.at[0, 0], o_sem.at[0])
    own_v = pltpu.make_async_copy(v_in, kv.at[0, 1], o_sem.at[1])
    own_k.start()
    own_v.start()
    doc_copy = pltpu.make_async_copy(doc_in, doc, d_sem)
    doc_copy.start()
    q_copy = pltpu.make_async_copy(q_in, qb, q_sem)
    q_copy.start()
    own_c = pltpu.make_async_copy(c_in, cb.at[t], c_sem)
    own_c.start()
    width = chunks * 256

    def w_copy(s):
        return pltpu.make_async_copy(
            w_in.at[:, pl.ds(pl.multiple_of(s * width, 256), width)], wb.at[s], w_sem.at[s]
        )

    for s in (t, partner, diag, cross):
        w_copy(s).start()

    with scope("barrier"):
        pl.semaphore_wait(barrier, 8)

    def send(src, dst, s_sem, r_sem, ctx, tp):
        return pltpu.make_async_remote_copy(
            src_ref=src,
            dst_ref=dst,
            send_sem=s_sem,
            recv_sem=r_sem,
            device_id=(ctx, tp),
            device_id_type=MESH,
        )

    def kv_send(src, place, b, ctx):
        return send(kv.at[src, b], kv.at[place, b], ks, kr.at[place, b], ctx, t)

    def far(place, b):
        return kv_send(0, place, b, ctx_at(4 * place))

    def near(src, place, e, b):
        return kv_send(src, place, b, peer(e))

    def arrived(place, b):
        near(0, place, 1, b).wait_recv()

    def cot_send(c, to, k):
        cols = pl.ds(c * 256, 256)
        return send(c_in.at[:, cols], cb.at[t, :, cols], cs, cr.at[k], i, to)

    def cot_pass(c):
        cols = pl.ds(c * 256, 256)
        block = cb.at[cross, :, cols]
        return send(block, block, cs, cr.at[6 if c < 3 else 7], i, partner)

    def cot_wait(s, lo, hi, k):
        block = cb.at[s, :, pl.ds(lo * 256, (hi - lo) * 256)]
        send(block, block, cs, cr.at[k], i, partner).wait_recv()

    for b, own in enumerate((own_k, own_v)):
        own.wait()
        far(1, b).start()
        far(2, b).start()
        for e in (1, 3):

            @pl.when(x + e < GROUP)
            def _():
                near(0, 2 + e, e, b).start()

    for c in range(chunks):
        cot_send(c, partner, 5).start()

    q_copy.wait()
    doc_copy.wait()
    for h in range(heads):
        q_head = qb[:, h * HEAD : (h + 1) * HEAD]
        qs[h] = q_head
        qt[h] = q_head.T

    lane = lax.broadcasted_iota(jnp.int32, (1, rows), 1)
    q_doc = jnp.where(lane < BLK, doc[2 * i], doc[2 * i + 1])

    def bias(d):
        src = ctx_at(-d)
        return [jnp.where(q_doc == doc[2 * src + b], 0.0, NEG) for b in range(2)]

    def scores(k, place, d):
        k_blk = kv[place, 0]
        if d is None:
            key = lax.broadcasted_iota(jnp.int32, (rows, rows), 0)
            query = lax.broadcasted_iota(jnp.int32, (rows, rows), 1)
            k_doc = jnp.where(key < BLK, doc[2 * i], doc[2 * i + 1])
            allowed = (key <= query) & (k_doc == q_doc)
        else:
            b0, b1 = bias(d)
        for h in range(heads):
            s = dot(k_blk, qt[h])
            if d is None:
                s = jnp.where(allowed, s, NEG)
            sb[k, h] = s
            top = jnp.max(s.reshape(2, BLK // 8, 8, rows), axis=1) * c2
            if d is None:
                top = jnp.maximum(top[0], top[1])
            else:
                top = jnp.maximum(top[0] + b0, top[1] + b1)
            m8[h] = top if k == 0 else jnp.maximum(m8[h], top)

    def weigh(group, entries):
        tops = []
        alphas = []
        for h in range(heads):
            m = jnp.max(m8[h], axis=0, keepdims=True)
            if group > 0:
                m = jnp.maximum(m, mrun[h])
                alphas.append(jnp.exp2(mrun[h] - m))
            mrun[h] = m
            mg[group, h] = m
            tops.append(m)
        v_t = jnp.concatenate([kv[place, 1].T for place, _ in entries], axis=1)
        shifts = [None if d is None else bias(d) for _, d in entries]
        for h in range(heads):
            blocks = []
            total = None
            for k, (place, d) in enumerate(entries):
                s = sb[k, h] * c2
                if d is None:
                    p = jnp.exp2(s - tops[h])
                else:
                    b0, b1 = shifts[k]
                    p = jnp.concatenate(
                        [jnp.exp2(s[:BLK] - (tops[h] - b0)), jnp.exp2(s[BLK:] - (tops[h] - b1))],
                        axis=0,
                    )
                part_sum = jnp.sum(p.reshape(rows // 8, 8, rows), axis=0)
                total = part_sum if total is None else total + part_sum
                p = p.astype(BF16)
                pb[place, h] = p
                blocks.append(p)
            out = dot(v_t, jnp.concatenate(blocks, axis=0))
            if group > 0:
                total = total + l8[h] * alphas[h]
                out = out + acc[h] * alphas[h]
            l8[h] = total
            acc[h] = out

    with scope("slot0"):
        scores(0, 0, None)
    for c in range(chunks):
        cot_send(c, cross, c).start()
    with scope("grad0"):
        w_copy(t).wait()
        own_c.wait()
        gt[...] = dot_t(wb[t], cb[t])
    for b in range(2):
        with scope("wait8"):
            arrived(2, b)

        @pl.when(x >= 2)
        def _():
            near(2, 6, 3, b).start()

        if b == 0:
            with scope("grad1"):
                w_copy(partner).wait()
                cot_wait(partner, 0, chunks, 5)
                gt[...] += dot_t(wb[partner], cb[partner])

    with scope("score8"):
        scores(2, 2, 8)
    for b in range(2):
        with scope("wait4"):
            arrived(1, b)

        for e in (1, 3):

            @pl.when(x + e < GROUP)
            def _():
                near(1, 3 + e, e, b).start()

            @pl.when(x + e >= GROUP)
            def _():
                near(1, 2 + e, e, b).start()

    for b in range(2):

        @pl.when(x == 1)
        def _():
            near(2, 6, 3, b).start()

        @pl.when(x == GROUP - 1)
        def _():
            near(2, 4, 1, b).start()

    with scope("score4"):
        scores(1, 1, 4)

    up, down = 3 + last, 6 - first
    for b in range(2):
        with scope("waitup"):
            arrived(up, b)
        near(up, 7, 1, b).start()
    with scope("groupA"):
        weigh(0, [(0, None), (1, 4), (2, 8)])
    for b in range(2):
        with scope("waitdown"):
            arrived(down, b)
        near(down, 8, -1, b).start()
    rest_up, rest_down = 4 - last, 5 + first
    group_b = [
        (up, 1 + 4 * last),
        (down, 7 - 4 * first),
        (rest_up, 5 - 4 * last),
        (rest_down, 3 + 4 * first),
    ]
    for k, (place, d) in enumerate(group_b):
        if k >= 2:
            with scope("waitb"):
                arrived(place, 0)
        with scope("scoreb"):
            scores(k, place, d)
    with scope("groupB"):
        arrived(rest_up, 1)
        arrived(rest_down, 1)
        weigh(1, group_b)
    for c in range(3):
        with scope("cotx"):
            cot_wait(cross, c, c + 1, c)
        cot_pass(c).start()

    def grad_piece(s, lo, hi):
        cols = slice(lo * 256, hi * 256)
        gt[...] += dot_t(wb[s, :, cols], cb[s, :, cols])

    with scope("grad2"):
        w_copy(cross).wait()
        grad_piece(cross, 0, 3)
    group_c = [(7, 2), (8, 6)]
    for k, (place, d) in enumerate(group_c):
        with scope("waitc"):
            arrived(place, 0)
        scores(k, place, d)
    with scope("groupC"):
        arrived(7, 1)
        arrived(8, 1)
        weigh(2, group_c)

        for h in range(heads):
            inv = 1.0 / jnp.sum(l8[h], axis=0, keepdims=True)
            linv[h] = inv
            a = (acc[h] * inv).astype(BF16)
            attn_t[h] = a
            attn[:, h * HEAD : (h + 1) * HEAD] = a.T

    def part(s, c):
        return dot(attn[...], wb[s, :, c * 256 : (c + 1) * 256])

    def to_partner(k, c):
        return send(pp.at[k, c], pr.at[k, c], ps, prs.at[chunks if k else c], i, partner)

    def to_cross(c):
        return send(xc.at[c], xr.at[c], xs, xrs, i, cross)

    with scope("diag"):
        w_copy(diag).wait()
        for c in range(chunks):
            pp[0, c] = part(diag, c).astype(BF16)
        for c in range(2):
            to_partner(0, c).start()
    for c in range(3, chunks):
        with scope("cotx"):
            cot_wait(cross, c, c + 1, c)
        cot_pass(c).start()
    for c in range(2, chunks):
        to_partner(0, c).start()

    def rs_step(lo, hi):
        with scope("rs1"):
            for c in range(lo, hi):
                to_partner(0, c).wait_recv()
                xc[c] = (po[c] + pr[0, c].astype(F32)).astype(BF16)
                to_cross(c).start()

    with scope("grad2"):
        grad_piece(cross, 3, chunks)
    with scope("cotd"):
        cot_wait(diag, 0, 3, 6)
    with scope("grad3"):
        grad_piece(diag, 0, 3)
    with scope("cross"):
        for c in range(chunks):
            po[c] = part(cross, c)
    rs_step(0, 2)
    with scope("cotd"):
        cot_wait(diag, 3, chunks, 7)
    with scope("grad3"):
        grad_piece(diag, 3, chunks)
    with scope("heads"):
        for h in range(heads):
            do_t = gt[h * HEAD : (h + 1) * HEAD].astype(BF16)
            dot_b[h] = do_t
            do_b[h] = do_t.T
            delta[h] = jnp.sum(do_t.astype(F32) * attn_t[h].astype(F32), axis=0, keepdims=True)

    def bwd_group(places, group):
        weights = [[] for _ in places]
        grads = [[] for _ in places]
        for h in range(heads):
            f = jnp.exp2(mg[group, h] - mrun[h]) * linv[h]
            for n, place in enumerate(places):
                p = pb[place, h].astype(F32) * f
                weights[n].append(p.astype(BF16))
                ds = (p * (dot(kv[place, 1], dot_b[h]) - delta[h])).astype(BF16)
                pb[place, h] = ds
                grads[n].append(ds)
        def values_part(n):
            w = jnp.concatenate(weights[n], axis=1)
            return dot(w, do_b[...].reshape(heads * rows, HEAD))

        def keys_part(n):
            ds = jnp.concatenate(grads[n], axis=1)
            return dot(ds, qs[...].reshape(heads * rows, HEAD)) * scale

        return keys_part, values_part

    def grad_relay(side, b):
        return send(
            gkv.at[7 + side, b],
            relay.at[side, b],
            gs,
            rr.at[side, b],
            peer(2 * side - 1),
            t,
        )

    def grad_near(side, j, b):
        return send(
            gkv.at[3 + 2 * side + j, b],
            rx.at[side, j, b],
            gs,
            gr.at[side, j, b],
            peer(2 * side - 1),
            t,
        )

    def bwd_step(k, carry):
        j_up = jnp.where(k == 1, 1 - last, last)
        j_down = jnp.where(k == 1, first, 1 - first)
        places = [jnp.where(k == 0, 7, 3 + j_up), jnp.where(k == 0, 8, 5 + j_down)]
        with scope("bwd"):
            parts = bwd_group(places, jnp.where(k == 0, 2, 1))
        for b in (1, 0):
            with scope("bwdpart"):
                done = [parts[b](n) for n in range(2)]

            @pl.when(k < 2)
            def _():
                for side, place in enumerate(places):
                    gkv[place, b] = done[side].astype(BF16)

            @pl.when(k == 2)
            def _():
                for side, place in enumerate(places):
                    with scope("waitrelay"):
                        grad_relay(side, b).wait_recv()
                    gkv[place, b] = (done[side] + relay[side, b].astype(F32)).astype(BF16)

            @pl.when(k == 0)
            def _():
                grad_relay(0, b).start()
                grad_relay(1, b).start()
                if b == 1:
                    rs_step(2, chunks)

            @pl.when(k > 0)
            def _():
                grad_near(0, j_up, b).start()
                grad_near(1, j_down, b).start()

        return carry

    lax.fori_loop(0, 3, bwd_step, 0)

    with scope("bwdown"):
        parts = bwd_group([0, 1, 2], 0)
        for n in range(3):
            for b in range(2):
                g3[n, b] = parts[b](n)

    with scope("partner"):
        for c in range(chunks):
            pp[1, c] = part(partner, c).astype(BF16)
        for c in range(chunks):
            to_partner(1, c).start()

    def grad_far(k, b):
        return send(
            gkv.at[k + 1, b], rz.at[k, b], gs, zr.at[k, b], ctx_at(-4 * k - 4), t
        )

    def near_sum(k, b):
        total = g3[k, b]
        for side, e in enumerate((1, 3)):
            j = k - lax.div(x + e, GROUP)
            block = rx[side, jnp.clip(j, 0, 1), b].astype(F32)
            total = total + jnp.where((j >= 0) & (j <= 1), block, 0.0)
        return total

    for b in (1, 0):
        with scope("gradnear"):
            for side in range(2):
                for j in range(2):
                    grad_near(side, j, b).wait_recv()
        with scope("nearsum"):
            for k in range(2):
                gkv[k + 1, b] = near_sum(k + 1, b).astype(BF16)
                grad_far(k, b).start()

    with scope("ownpart"):
        for c in range(chunks):
            po[c] = part(t, c)
    for b in range(2):
        g3[0, b] = near_sum(0, b)

    def put(n):
        src = (mixed, gq, gv, gk)[n]
        dst = (mixed_out, gq_out, gv_out, gk_out)[n]
        return pltpu.make_async_copy(src, dst, out_sem.at[n])

    with scope("dq"):
        for n in range(SLOTS):
            ktb[:, n * rows : (n + 1) * rows] = kv[n, 0].T
        for h in range(heads):
            dq_t = dot(ktb[...], pb[:, h].reshape(SLOTS * rows, rows))
            gq[:, h * HEAD : (h + 1) * HEAD] = (dq_t * scale).T.astype(BF16)
    put(1).start()
    with scope("rscross"):
        send(pp.at[1], pr.at[1], ps, prs.at[chunks], i, partner).wait_recv()
        send(xc, xr, xs, xrs, i, cross).wait_recv()
    for c in range(chunks):
        mixed[:, c * 256 : (c + 1) * 256] = (
            po[c] + pr[1, c].astype(F32) + xr[c].astype(F32)
        ).astype(BF16)
    put(0).start()
    with scope("sent"):
        block = kv.at[pl.ds(1, SLOTS - 1)]
        send(block, block, ks, kr.at[0, 0], i, partner).wait_send()
        block = cb.at[pl.ds(0, 3)]
        send(block, block, cs, cr.at[0], i, partner).wait_send()
        send(pp, pr, ps, prs.at[0], i, partner).wait_send()
        send(xc, xr, xs, xrs, i, cross).wait_send()
    for b, result in ((1, gv), (0, gk)):
        for k in range(2):
            with scope("gradfar"):
                grad_far(k, b).wait_recv()
        result[...] = (g3[0, b] + rz[0, b].astype(F32) + rz[1, b].astype(F32)).astype(BF16)
        put(3 - b).start()

    with scope("put"):
        for n in range(4):
            put(n).wait()
        block = gkv.at[pl.ds(1, SLOTS - 1)]
        send(block, block, gs, zr.at[0, 0], i, partner).wait_send()


def leave(*refs):
    count = (len(refs) - 1) // 2
    sem = refs[-1]
    copies = [
        pltpu.make_async_copy(refs[n], refs[count + n], sem.at[n]) for n in range(count)
    ]
    for copy in copies:
        copy.start()
    for copy in copies:
        copy.wait()


def on_device(queries, keys, values, out_weight, cotangent, doc_ids):
    n_ctx = lax.axis_size("ctx")
    rows = queries.shape[0]
    heads = queries.shape[1] // HEAD
    chunks = cotangent.shape[1] // 256
    any_space = pl.BlockSpec(memory_space=pl.ANY)
    hbm = pl.BlockSpec(memory_space=pltpu.HBM)
    dma = pltpu.SemaphoreType.DMA
    shapes = tuple(
        jax.ShapeDtypeStruct(like.shape, BF16) for like in (cotangent, queries, keys, values)
    )
    results = pl.pallas_call(
        functools.partial(kernel, n_ctx, heads, rows, chunks),
        out_shape=shapes,
        in_specs=[hbm] * 6,
        out_specs=(any_space,) * 4,
        scratch_shapes=[
            *[pltpu.VMEM(shape.shape, BF16) for shape in shapes],
            dma((4,)),
            pltpu.SMEM(doc_ids.shape, jnp.int32),
            pltpu.VMEM((rows, heads * HEAD), BF16),
            pltpu.VMEM((heads, rows, HEAD), BF16),
            pltpu.VMEM((SLOTS, 2, rows, HEAD), BF16),
            pltpu.VMEM((4, heads * HEAD, chunks * 256), BF16),
            pltpu.VMEM((4, rows, chunks * 256), BF16),
            pltpu.VMEM((heads, HEAD, rows), BF16),
            pltpu.VMEM((4, heads, rows, rows), F32),
            pltpu.VMEM((SLOTS, heads, rows, rows), BF16),
            pltpu.VMEM((3, heads, 1, rows), F32),
            pltpu.VMEM((heads, 8, rows), F32),
            pltpu.VMEM((heads, 1, rows), F32),
            pltpu.VMEM((heads, 8, rows), F32),
            pltpu.VMEM((heads, 1, rows), F32),
            pltpu.VMEM((heads, HEAD, rows), F32),
            pltpu.VMEM((heads, HEAD, rows), BF16),
            pltpu.VMEM((rows, heads * HEAD), BF16),
            pltpu.VMEM((heads * HEAD, rows), F32),
            pltpu.VMEM((heads, HEAD, rows), BF16),
            pltpu.VMEM((heads, rows, HEAD), BF16),
            pltpu.VMEM((heads, 1, rows), F32),
            pltpu.VMEM((HEAD, SLOTS * rows), BF16),
            pltpu.VMEM((SLOTS, 2, rows, HEAD), BF16),
            pltpu.VMEM((3, 2, rows, HEAD), F32),
            pltpu.VMEM((2, 2, rows, HEAD), BF16),
            pltpu.VMEM((2, 2, 2, rows, HEAD), BF16),
            pltpu.VMEM((2, 2, rows, HEAD), BF16),
            pltpu.VMEM((2, chunks, rows, 256), BF16),
            pltpu.VMEM((2, chunks, rows, 256), BF16),
            pltpu.VMEM((chunks, rows, 256), BF16),
            pltpu.VMEM((chunks, rows, 256), BF16),
            pltpu.VMEM((chunks, rows, 256), F32),
            dma,
            dma,
            dma((2,)),
            dma((4,)),
            dma,
            dma,
            dma((SLOTS, 2)),
            dma,
            dma((8,)),
            dma((2, 2)),
            dma,
            dma((2, 2, 2)),
            dma((2, 2)),
            dma,
            dma((chunks + 1,)),
            dma,
            dma,
        ],
        compiler_params=pltpu.CompilerParams(
            collective_id=0, has_side_effects=True, vmem_limit_bytes=50 * 1024 * 1024
        ),
    )(
        *[
            pltpu.with_memory_space_constraint(a, pltpu.HBM)
            for a in (doc_ids, queries, keys, values, out_weight, cotangent)
        ]
    )
    return pl.pallas_call(
        leave,
        out_shape=shapes,
        in_specs=[any_space] * 4,
        out_specs=(any_space,) * 4,
        scratch_shapes=[dma((4,))],
        compiler_params=pltpu.CompilerParams(vmem_limit_bytes=1024 * 1024),
    )(*results)


def solution(mesh):
    return jax.shard_map(
        on_device,
        mesh=mesh,
        in_specs=(
            P("ctx", "tp"),
            P("ctx", "tp"),
            P("ctx", "tp"),
            P("tp", None),
            P("ctx", "tp"),
            P(),
        ),
        out_specs=(P("ctx", "tp"), P("ctx", "tp"), P("ctx", "tp"), P("ctx", "tp")),
        check_vma=False,
    )
```

```python
import contextlib
import functools
import math

import jax
import jax.numpy as jnp
from jax import lax
from jax.experimental import pallas as pl
from jax.experimental.pallas import tpu as pltpu
from jax.sharding import PartitionSpec as P

HEAD = 128
BLK = 128
GROUP = 4
SLOTS = 2 * GROUP + 1
NEG = -1e30
F32 = jnp.float32
BF16 = jnp.bfloat16
MESH = pl.DeviceIdType.MESH


def dot(a, b):
    return lax.dot_general(a, b, (((1,), (0,)), ((), ())), preferred_element_type=F32)


def dot_t(a, b):
    return lax.dot_general(a, b, (((1,), (1,)), ((), ())), preferred_element_type=F32)


def scope(name):
    return contextlib.nullcontext()


def kernel(
    n_ctx,
    heads,
    rows,
    chunks,
    doc_in,
    q_in,
    k_in,
    v_in,
    w_in,
    c_in,
    mixed_out,
    gq_out,
    gk_out,
    gv_out,
    mixed,
    gq,
    gk,
    gv,
    out_sem,
    doc,
    qb,
    qs,
    kv,
    wb,
    cb,
    qt,
    sb,
    pb,
    mg,
    m8,
    mrun,
    l8,
    linv,
    acc,
    attn_t,
    attn,
    gt,
    dot_b,
    do_b,
    delta,
    ktb,
    gkv,
    g3,
    relay,
    rx,
    rz,
    pp,
    pr,
    xc,
    xr,
    po,
    d_sem,
    q_sem,
    o_sem,
    w_sem,
    c_sem,
    ks,
    kp,
    kr,
    cs,
    cr,
    rr,
    gs,
    gr,
    zr,
    ps,
    prs,
    xs,
    xrs,
):
    i = lax.axis_index("ctx")
    t = lax.axis_index("tp")
    x = lax.rem(i, GROUP)
    g0 = i - x
    partner = t + 1 - 2 * lax.rem(t, 2)
    cross = lax.rem(t + 2, 4)
    diag = lax.rem(partner + 2, 4)
    scale = 1.0 / math.sqrt(HEAD)
    c2 = scale * math.log2(math.e)
    last = lax.div(x, GROUP - 1)
    first = lax.div(GROUP - 1 - x, GROUP - 1)

    def ctx_at(by):
        return lax.rem(i + by + n_ctx, n_ctx)

    def peer(e):
        return g0 + lax.rem(x + e + GROUP, GROUP)

    barrier = pltpu.get_barrier_semaphore()
    for by in (4, -4, 8, -8):
        pl.semaphore_signal(barrier, inc=1, device_id=(ctx_at(by), t), device_id_type=MESH)
    for e in (1, 2, 3):
        pl.semaphore_signal(barrier, inc=1, device_id=(peer(e), t), device_id_type=MESH)
    for other in (partner, cross):
        pl.semaphore_signal(barrier, inc=1, device_id=(i, other), device_id_type=MESH)

    own_k = pltpu.make_async_copy(k_in, kv.at[0, 0], o_sem.at[0])
    own_v = pltpu.make_async_copy(v_in, kv.at[0, 1], o_sem.at[1])
    own_k.start()
    own_v.start()
    doc_copy = pltpu.make_async_copy(doc_in, doc, d_sem)
    doc_copy.start()
    q_copy = pltpu.make_async_copy(q_in, qb, q_sem)
    q_copy.start()
    own_c = pltpu.make_async_copy(c_in, cb.at[t], c_sem)
    own_c.start()
    width = chunks * 256

    def w_copy(s):
        return pltpu.make_async_copy(
            w_in.at[:, pl.ds(pl.multiple_of(s * width, 256), width)], wb.at[s], w_sem.at[s]
        )

    for s in (t, partner, diag, cross):
        w_copy(s).start()

    with scope("barrier"):
        pl.semaphore_wait(barrier, 9)

    def send(src, dst, s_sem, r_sem, ctx, tp):
        return pltpu.make_async_remote_copy(
            src_ref=src,
            dst_ref=dst,
            send_sem=s_sem,
            recv_sem=r_sem,
            device_id=(ctx, tp),
            device_id_type=MESH,
        )

    def kv_send(src, place, b, ctx):
        return send(kv.at[src, b], kv.at[place, b], ks, kr.at[place, b], ctx, t)

    def far(place, b):
        return kv_send(0, place, b, ctx_at(4 * place))

    def near(src, place, e, b):
        return kv_send(src, place, b, peer(e))

    def pass_on(src, place, e, b):
        block = kv.at[place, b]
        return send(kv.at[src, b], block, kp.at[place - 7, b], kr.at[place, b], peer(e), t)

    middle = (x >= 1) & (x <= 2)

    def arrived(place, b):
        near(0, place, 1, b).wait_recv()

    def cot_send(c, to, k):
        cols = pl.ds(c * 256, 256)
        return send(c_in.at[:, cols], cb.at[t, :, cols], cs, cr.at[k], i, to)

    def cot_pass(c):
        cols = pl.ds(c * 256, 256)
        block = cb.at[cross, :, cols]
        return send(block, block, cs, cr.at[6 if c < 3 else 7], i, partner)

    def cot_wait(s, lo, hi, k):
        block = cb.at[s, :, pl.ds(lo * 256, (hi - lo) * 256)]
        send(block, block, cs, cr.at[k], i, partner).wait_recv()

    for b, own in enumerate((own_k, own_v)):
        own.wait()
        far(1, b).start()
        far(2, b).start()
        for e in (1, 3):

            @pl.when(x + e < GROUP)
            def _():
                near(0, 2 + e, e, b).start()

    for c in range(chunks):
        cot_send(c, partner, 5).start()

    q_copy.wait()
    doc_copy.wait()
    for h in range(heads):
        q_head = qb[:, h * HEAD : (h + 1) * HEAD]
        qs[h] = q_head
        qt[h] = q_head.T

    lane = lax.broadcasted_iota(jnp.int32, (1, rows), 1)
    q_doc = jnp.where(lane < BLK, doc[2 * i], doc[2 * i + 1])

    def bias(d):
        src = ctx_at(-d)
        return [jnp.where(q_doc == doc[2 * src + b], 0.0, NEG) for b in range(2)]

    def scores(k, place, d):
        k_blk = kv[place, 0]
        if d is None:
            key = lax.broadcasted_iota(jnp.int32, (rows, rows), 0)
            query = lax.broadcasted_iota(jnp.int32, (rows, rows), 1)
            k_doc = jnp.where(key < BLK, doc[2 * i], doc[2 * i + 1])
            allowed = (key <= query) & (k_doc == q_doc)
        else:
            b0, b1 = bias(d)
        for h in range(heads):
            s = dot(k_blk, qt[h])
            if d is None:
                s = jnp.where(allowed, s, NEG)
            sb[k, h] = s
            top = jnp.max(s.reshape(2, BLK // 8, 8, rows), axis=1) * c2
            if d is None:
                top = jnp.maximum(top[0], top[1])
            else:
                top = jnp.maximum(top[0] + b0, top[1] + b1)
            m8[h] = top if k == 0 else jnp.maximum(m8[h], top)

    def weigh(group, entries):
        tops = []
        alphas = []
        for h in range(heads):
            m = jnp.max(m8[h], axis=0, keepdims=True)
            if group > 0:
                m = jnp.maximum(m, mrun[h])
                alphas.append(jnp.exp2(mrun[h] - m))
            mrun[h] = m
            mg[group, h] = m
            tops.append(m)
        v_t = jnp.concatenate([kv[place, 1].T for place, _ in entries], axis=1)
        shifts = [None if d is None else bias(d) for _, d in entries]
        for h in range(heads):
            blocks = []
            total = None
            for k, (place, d) in enumerate(entries):
                s = sb[k, h] * c2
                if d is None:
                    p = jnp.exp2(s - tops[h])
                else:
                    b0, b1 = shifts[k]
                    p = jnp.concatenate(
                        [jnp.exp2(s[:BLK] - (tops[h] - b0)), jnp.exp2(s[BLK:] - (tops[h] - b1))],
                        axis=0,
                    )
                part_sum = jnp.sum(p.reshape(rows // 8, 8, rows), axis=0)
                total = part_sum if total is None else total + part_sum
                p = p.astype(BF16)
                pb[place, h] = p
                blocks.append(p)
            out = dot(v_t, jnp.concatenate(blocks, axis=0))
            if group > 0:
                total = total + l8[h] * alphas[h]
                out = out + acc[h] * alphas[h]
            l8[h] = total
            acc[h] = out

    with scope("slot0"):
        scores(0, 0, None)
    for c in range(chunks):
        cot_send(c, cross, c).start()
    with scope("grad0"):
        w_copy(t).wait()
        own_c.wait()
        gt[...] = dot_t(wb[t], cb[t])
    for b in range(2):
        with scope("wait8"):
            arrived(2, b)

        @pl.when(x >= 2)
        def _():
            near(2, 6, 3, b).start()

        if b == 0:
            with scope("grad1"):
                w_copy(partner).wait()
                cot_wait(partner, 0, chunks, 5)
                gt[...] += dot_t(wb[partner], cb[partner])

    for b in range(2):

        @pl.when(middle)
        def _():
            arrived(3, b)
            pass_on(3, 7, 1, b).start()

    with scope("score8"):
        scores(2, 2, 8)
    for b in range(2):
        with scope("wait4"):
            arrived(1, b)

        for e in (1, 3):

            @pl.when(x + e < GROUP)
            def _():
                near(1, 3 + e, e, b).start()

            @pl.when(x + e >= GROUP)
            def _():
                near(1, 2 + e, e, b).start()

        near(1, 8 - lax.div(x, 2), 2, b).start()

    for b in range(2):

        @pl.when(x == 1)
        def _():
            near(2, 6, 3, b).start()

        @pl.when(x == GROUP - 1)
        def _():
            near(2, 4, 1, b).start()

    with scope("score4"):
        scores(1, 1, 4)

    up, down = 3 + last, 6 - first
    for b in range(2):

        @pl.when(middle)
        def _():
            arrived(6, b)
            pass_on(6, 8, -1, b).start()

    with scope("groupA"):
        weigh(0, [(0, None), (1, 4), (2, 8)])
    for b in range(2):

        @pl.when(jnp.logical_not(middle))
        def _():
            arrived(up, b)
            arrived(down, b)

    rest_up, rest_down = 4 - last, 5 + first
    group_b = [
        (up, 1 + 4 * last),
        (down, 7 - 4 * first),
        (rest_up, 5 - 4 * last),
        (rest_down, 3 + 4 * first),
    ]
    for k, (place, d) in enumerate(group_b):
        if k >= 2:
            with scope("waitb"):
                arrived(place, 0)
        with scope("scoreb"):
            scores(k, place, d)
    with scope("groupB"):
        arrived(rest_up, 1)
        arrived(rest_down, 1)
        weigh(1, group_b)
    for c in range(3):
        with scope("cotx"):
            cot_wait(cross, c, c + 1, c)
        cot_pass(c).start()

    def grad_piece(s, lo, hi):
        cols = slice(lo * 256, hi * 256)
        gt[...] += dot_t(wb[s, :, cols], cb[s, :, cols])

    with scope("grad2"):
        w_copy(cross).wait()
        grad_piece(cross, 0, 3)
    group_c = [(7, 2), (8, 6)]
    for k, (place, d) in enumerate(group_c):
        with scope("waitc"):
            arrived(place, 0)
        scores(k, place, d)
    with scope("groupC"):
        arrived(7, 1)
        arrived(8, 1)
        weigh(2, group_c)

        for h in range(heads):
            inv = 1.0 / jnp.sum(l8[h], axis=0, keepdims=True)
            linv[h] = inv
            a = (acc[h] * inv).astype(BF16)
            attn_t[h] = a
            attn[:, h * HEAD : (h + 1) * HEAD] = a.T

    def part(s, c):
        return dot(attn[...], wb[s, :, c * 256 : (c + 1) * 256])

    def to_partner(k, c):
        return send(pp.at[k, c], pr.at[k, c], ps, prs.at[chunks if k else c], i, partner)

    def to_cross(c):
        return send(xc.at[c], xr.at[c], xs, xrs, i, cross)

    with scope("diag"):
        w_copy(diag).wait()
        for c in range(chunks):
            pp[0, c] = part(diag, c).astype(BF16)
        for c in range(2):
            to_partner(0, c).start()
    for c in range(3, chunks):
        with scope("cotx"):
            cot_wait(cross, c, c + 1, c)
        cot_pass(c).start()
    for c in range(2, chunks):
        to_partner(0, c).start()

    def rs_step(lo, hi):
        with scope("rs1"):
            for c in range(lo, hi):
                to_partner(0, c).wait_recv()
                xc[c] = (po[c] + pr[0, c].astype(F32)).astype(BF16)
                to_cross(c).start()

    with scope("grad2"):
        grad_piece(cross, 3, chunks)
    with scope("cotd"):
        cot_wait(diag, 0, 3, 6)
    with scope("grad3"):
        grad_piece(diag, 0, 3)
    with scope("cross"):
        for c in range(chunks):
            po[c] = part(cross, c)
    rs_step(0, 2)
    with scope("cotd"):
        cot_wait(diag, 3, chunks, 7)
    with scope("grad3"):
        grad_piece(diag, 3, chunks)
    with scope("heads"):
        for h in range(heads):
            do_t = gt[h * HEAD : (h + 1) * HEAD].astype(BF16)
            dot_b[h] = do_t
            do_b[h] = do_t.T
            delta[h] = jnp.sum(do_t.astype(F32) * attn_t[h].astype(F32), axis=0, keepdims=True)

    def bwd_group(places, group):
        weights = [[] for _ in places]
        grads = [[] for _ in places]
        for h in range(heads):
            f = jnp.exp2(mg[group, h] - mrun[h]) * linv[h]
            for n, place in enumerate(places):
                p = pb[place, h].astype(F32) * f
                weights[n].append(p.astype(BF16))
                ds = (p * (dot(kv[place, 1], dot_b[h]) - delta[h])).astype(BF16)
                pb[place, h] = ds
                grads[n].append(ds)
        def values_part(n):
            w = jnp.concatenate(weights[n], axis=1)
            return dot(w, do_b[...].reshape(heads * rows, HEAD))

        def keys_part(n):
            ds = jnp.concatenate(grads[n], axis=1)
            return dot(ds, qs[...].reshape(heads * rows, HEAD)) * scale

        return keys_part, values_part

    def grad_relay(side, b):
        return send(
            gkv.at[7 + side, b],
            relay.at[side, b],
            gs,
            rr.at[side, b],
            peer(2 * side - 1),
            t,
        )

    def grad_near(side, j, b):
        return send(
            gkv.at[3 + 2 * side + j, b],
            rx.at[side, j, b],
            gs,
            gr.at[side, j, b],
            peer(2 * side - 1),
            t,
        )

    def bwd_step(k, carry):
        j_up = jnp.where(k == 1, 1 - last, last)
        j_down = jnp.where(k == 1, first, 1 - first)
        places = [jnp.where(k == 0, 7, 3 + j_up), jnp.where(k == 0, 8, 5 + j_down)]
        with scope("bwd"):
            parts = bwd_group(places, jnp.where(k == 0, 2, 1))
        for b in (1, 0):
            with scope("bwdpart"):
                done = [parts[b](n) for n in range(2)]

            @pl.when(k < 2)
            def _():
                for side, place in enumerate(places):
                    gkv[place, b] = done[side].astype(BF16)

            @pl.when(k == 2)
            def _():
                for side, place in enumerate(places):
                    with scope("waitrelay"):
                        grad_relay(side, b).wait_recv()
                    gkv[place, b] = (done[side] + relay[side, b].astype(F32)).astype(BF16)

            @pl.when(k == 0)
            def _():
                grad_relay(0, b).start()
                grad_relay(1, b).start()
                if b == 1:
                    rs_step(2, chunks)

            @pl.when(k > 0)
            def _():
                grad_near(0, j_up, b).start()
                grad_near(1, j_down, b).start()

        return carry

    lax.fori_loop(0, 3, bwd_step, 0)

    with scope("bwdown"):
        parts = bwd_group([0, 1, 2], 0)
        for n in range(3):
            for b in range(2):
                g3[n, b] = parts[b](n)

    with scope("partner"):
        for c in range(chunks):
            pp[1, c] = part(partner, c).astype(BF16)
        for c in range(chunks):
            to_partner(1, c).start()

    def grad_far(k, b):
        return send(
            gkv.at[k + 1, b], rz.at[k, b], gs, zr.at[k, b], ctx_at(-4 * k - 4), t
        )

    def near_sum(k, b):
        total = g3[k, b]
        for side, e in enumerate((1, 3)):
            j = k - lax.div(x + e, GROUP)
            block = rx[side, jnp.clip(j, 0, 1), b].astype(F32)
            total = total + jnp.where((j >= 0) & (j <= 1), block, 0.0)
        return total

    for b in (1, 0):
        with scope("gradnear"):
            for side in range(2):
                for j in range(2):
                    grad_near(side, j, b).wait_recv()
        with scope("nearsum"):
            for k in range(2):
                gkv[k + 1, b] = near_sum(k + 1, b).astype(BF16)
                grad_far(k, b).start()

    with scope("ownpart"):
        for c in range(chunks):
            po[c] = part(t, c)
    for b in range(2):
        g3[0, b] = near_sum(0, b)

    def put(n):
        src = (mixed, gq, gv, gk)[n]
        dst = (mixed_out, gq_out, gv_out, gk_out)[n]
        return pltpu.make_async_copy(src, dst, out_sem.at[n])

    with scope("dq"):
        for n in range(SLOTS):
            ktb[:, n * rows : (n + 1) * rows] = kv[n, 0].T
        for h in range(heads):
            dq_t = dot(ktb[...], pb[:, h].reshape(SLOTS * rows, rows))
            gq[:, h * HEAD : (h + 1) * HEAD] = (dq_t * scale).T.astype(BF16)
    put(1).start()
    with scope("rscross"):
        send(pp.at[1], pr.at[1], ps, prs.at[chunks], i, partner).wait_recv()
        send(xc, xr, xs, xrs, i, cross).wait_recv()
    for c in range(chunks):
        mixed[:, c * 256 : (c + 1) * 256] = (
            po[c] + pr[1, c].astype(F32) + xr[c].astype(F32)
        ).astype(BF16)
    put(0).start()
    with scope("sent"):
        block = kv.at[pl.ds(1, SLOTS - 2)]
        send(block, block, ks, kr.at[0, 0], i, partner).wait_send()

        @pl.when(middle)
        def _():
            for b in range(2):
                pass_on(3, 7, 1, b).wait_send()
                pass_on(6, 8, -1, b).wait_send()

        block = cb.at[pl.ds(0, 3)]
        send(block, block, cs, cr.at[0], i, partner).wait_send()
        send(pp, pr, ps, prs.at[0], i, partner).wait_send()
        send(xc, xr, xs, xrs, i, cross).wait_send()
    for b, result in ((1, gv), (0, gk)):
        for k in range(2):
            with scope("gradfar"):
                grad_far(k, b).wait_recv()
        result[...] = (g3[0, b] + rz[0, b].astype(F32) + rz[1, b].astype(F32)).astype(BF16)
        put(3 - b).start()

    with scope("put"):
        for n in range(4):
            put(n).wait()
        block = gkv.at[pl.ds(1, SLOTS - 1)]
        send(block, block, gs, zr.at[0, 0], i, partner).wait_send()


def leave(*refs):
    count = (len(refs) - 1) // 2
    sem = refs[-1]
    copies = [
        pltpu.make_async_copy(refs[n], refs[count + n], sem.at[n]) for n in range(count)
    ]
    for copy in copies:
        copy.start()
    for copy in copies:
        copy.wait()


def on_device(queries, keys, values, out_weight, cotangent, doc_ids):
    n_ctx = lax.axis_size("ctx")
    rows = queries.shape[0]
    heads = queries.shape[1] // HEAD
    chunks = cotangent.shape[1] // 256
    any_space = pl.BlockSpec(memory_space=pl.ANY)
    hbm = pl.BlockSpec(memory_space=pltpu.HBM)
    dma = pltpu.SemaphoreType.DMA
    shapes = tuple(
        jax.ShapeDtypeStruct(like.shape, BF16) for like in (cotangent, queries, keys, values)
    )
    results = pl.pallas_call(
        functools.partial(kernel, n_ctx, heads, rows, chunks),
        out_shape=shapes,
        in_specs=[hbm] * 6,
        out_specs=(any_space,) * 4,
        scratch_shapes=[
            *[pltpu.VMEM(shape.shape, BF16) for shape in shapes],
            dma((4,)),
            pltpu.SMEM(doc_ids.shape, jnp.int32),
            pltpu.VMEM((rows, heads * HEAD), BF16),
            pltpu.VMEM((heads, rows, HEAD), BF16),
            pltpu.VMEM((SLOTS, 2, rows, HEAD), BF16),
            pltpu.VMEM((4, heads * HEAD, chunks * 256), BF16),
            pltpu.VMEM((4, rows, chunks * 256), BF16),
            pltpu.VMEM((heads, HEAD, rows), BF16),
            pltpu.VMEM((4, heads, rows, rows), F32),
            pltpu.VMEM((SLOTS, heads, rows, rows), BF16),
            pltpu.VMEM((3, heads, 1, rows), F32),
            pltpu.VMEM((heads, 8, rows), F32),
            pltpu.VMEM((heads, 1, rows), F32),
            pltpu.VMEM((heads, 8, rows), F32),
            pltpu.VMEM((heads, 1, rows), F32),
            pltpu.VMEM((heads, HEAD, rows), F32),
            pltpu.VMEM((heads, HEAD, rows), BF16),
            pltpu.VMEM((rows, heads * HEAD), BF16),
            pltpu.VMEM((heads * HEAD, rows), F32),
            pltpu.VMEM((heads, HEAD, rows), BF16),
            pltpu.VMEM((heads, rows, HEAD), BF16),
            pltpu.VMEM((heads, 1, rows), F32),
            pltpu.VMEM((HEAD, SLOTS * rows), BF16),
            pltpu.VMEM((SLOTS, 2, rows, HEAD), BF16),
            pltpu.VMEM((3, 2, rows, HEAD), F32),
            pltpu.VMEM((2, 2, rows, HEAD), BF16),
            pltpu.VMEM((2, 2, 2, rows, HEAD), BF16),
            pltpu.VMEM((2, 2, rows, HEAD), BF16),
            pltpu.VMEM((2, chunks, rows, 256), BF16),
            pltpu.VMEM((2, chunks, rows, 256), BF16),
            pltpu.VMEM((chunks, rows, 256), BF16),
            pltpu.VMEM((chunks, rows, 256), BF16),
            pltpu.VMEM((chunks, rows, 256), F32),
            dma,
            dma,
            dma((2,)),
            dma((4,)),
            dma,
            dma,
            dma((2, 2)),
            dma((SLOTS, 2)),
            dma,
            dma((8,)),
            dma((2, 2)),
            dma,
            dma((2, 2, 2)),
            dma((2, 2)),
            dma,
            dma((chunks + 1,)),
            dma,
            dma,
        ],
        compiler_params=pltpu.CompilerParams(
            collective_id=0, has_side_effects=True, vmem_limit_bytes=50 * 1024 * 1024
        ),
    )(
        *[
            pltpu.with_memory_space_constraint(a, pltpu.HBM)
            for a in (doc_ids, queries, keys, values, out_weight, cotangent)
        ]
    )
    return pl.pallas_call(
        leave,
        out_shape=shapes,
        in_specs=[any_space] * 4,
        out_specs=(any_space,) * 4,
        scratch_shapes=[dma((4,))],
        compiler_params=pltpu.CompilerParams(vmem_limit_bytes=1024 * 1024),
    )(*results)


def solution(mesh):
    return jax.shard_map(
        on_device,
        mesh=mesh,
        in_specs=(
            P("ctx", "tp"),
            P("ctx", "tp"),
            P("ctx", "tp"),
            P("tp", None),
            P("ctx", "tp"),
            P(),
        ),
        out_specs=(P("ctx", "tp"), P("ctx", "tp"), P("ctx", "tp"), P("ctx", "tp")),
        check_vma=False,
    )
```

```python
import contextlib
import functools
import math

import jax
import jax.numpy as jnp
from jax import lax
from jax.experimental import pallas as pl
from jax.experimental.pallas import tpu as pltpu
from jax.sharding import PartitionSpec as P

HEAD = 128
BLK = 128
GROUP = 4
SLOTS = 2 * GROUP + 1
NEG = -1e30
F32 = jnp.float32
BF16 = jnp.bfloat16
MESH = pl.DeviceIdType.MESH


def dot(a, b):
    return lax.dot_general(a, b, (((1,), (0,)), ((), ())), preferred_element_type=F32)


def dot_t(a, b):
    return lax.dot_general(a, b, (((1,), (1,)), ((), ())), preferred_element_type=F32)


def scope(name):
    return contextlib.nullcontext()


def kernel(
    n_ctx,
    heads,
    rows,
    chunks,
    doc_in,
    q_in,
    k_in,
    v_in,
    w_in,
    c_in,
    mixed_out,
    gq_out,
    gk_out,
    gv_out,
    mixed,
    gq,
    gk,
    gv,
    out_sem,
    doc,
    qb,
    qs,
    kv,
    wb,
    cb,
    qt,
    sb,
    pb,
    mg,
    m8,
    mrun,
    l8,
    linv,
    acc,
    attn_t,
    attn,
    gt,
    dot_b,
    do_b,
    delta,
    ktb,
    gkv,
    g3,
    relay,
    rx,
    rz,
    pp,
    pr,
    xc,
    xr,
    po,
    d_sem,
    q_sem,
    o_sem,
    w_sem,
    c_sem,
    ks,
    kr,
    cs,
    cr,
    rr,
    gs,
    gr,
    zr,
    ps,
    prs,
    xs,
    xrs,
):
    i = lax.axis_index("ctx")
    t = lax.axis_index("tp")
    x = lax.rem(i, GROUP)
    g0 = i - x
    partner = t + 1 - 2 * lax.rem(t, 2)
    cross = lax.rem(t + 2, 4)
    diag = lax.rem(partner + 2, 4)
    scale = 1.0 / math.sqrt(HEAD)
    c2 = scale * math.log2(math.e)
    last = lax.div(x, GROUP - 1)
    first = lax.div(GROUP - 1 - x, GROUP - 1)

    def ctx_at(by):
        return lax.rem(i + by + n_ctx, n_ctx)

    def peer(e):
        return g0 + lax.rem(x + e + GROUP, GROUP)

    barrier = pltpu.get_barrier_semaphore()
    for by in (4, -4, 8, -8):
        pl.semaphore_signal(barrier, inc=1, device_id=(ctx_at(by), t), device_id_type=MESH)
    for e in (1, 3):
        pl.semaphore_signal(barrier, inc=1, device_id=(peer(e), t), device_id_type=MESH)
    for other in (partner, cross):
        pl.semaphore_signal(barrier, inc=1, device_id=(i, other), device_id_type=MESH)

    own_k = pltpu.make_async_copy(k_in, kv.at[0, 0], o_sem.at[0])
    own_v = pltpu.make_async_copy(v_in, kv.at[0, 1], o_sem.at[1])
    own_k.start()
    own_v.start()
    doc_copy = pltpu.make_async_copy(doc_in, doc, d_sem)
    doc_copy.start()
    q_copy = pltpu.make_async_copy(q_in, qb, q_sem)
    q_copy.start()
    own_c = pltpu.make_async_copy(c_in, cb.at[t], c_sem)
    own_c.start()
    width = chunks * 256

    def w_copy(s):
        return pltpu.make_async_copy(
            w_in.at[:, pl.ds(pl.multiple_of(s * width, 256), width)], wb.at[s], w_sem.at[s]
        )

    for s in (t, partner, diag, cross):
        w_copy(s).start()

    with scope("barrier"):
        pl.semaphore_wait(barrier, 8)

    def send(src, dst, s_sem, r_sem, ctx, tp):
        return pltpu.make_async_remote_copy(
            src_ref=src,
            dst_ref=dst,
            send_sem=s_sem,
            recv_sem=r_sem,
            device_id=(ctx, tp),
            device_id_type=MESH,
        )

    def kv_send(src, place, b, ctx):
        return send(kv.at[src, b], kv.at[place, b], ks, kr.at[place, b], ctx, t)

    def far(place, b):
        return kv_send(0, place, b, ctx_at(4 * place))

    def near(src, place, e, b):
        return kv_send(src, place, b, peer(e))

    def arrived(place, b):
        near(0, place, 1, b).wait_recv()

    def cot_send(c, to, k):
        cols = pl.ds(c * 256, 256)
        return send(c_in.at[:, cols], cb.at[t, :, cols], cs, cr.at[k], i, to)

    def cot_pass(c):
        cols = pl.ds(c * 256, 256)
        block = cb.at[cross, :, cols]
        return send(block, block, cs, cr.at[6 if c < 3 else 7], i, partner)

    def cot_wait(s, lo, hi, k):
        block = cb.at[s, :, pl.ds(lo * 256, (hi - lo) * 256)]
        send(block, block, cs, cr.at[k], i, partner).wait_recv()

    for b, own in enumerate((own_k, own_v)):
        own.wait()
        far(1, b).start()
        far(2, b).start()
        for e in (1, 3):

            @pl.when(x + e < GROUP)
            def _():
                near(0, 2 + e, e, b).start()

    for c in range(chunks):
        cot_send(c, partner, 5).start()

    q_copy.wait()
    doc_copy.wait()
    for h in range(heads):
        q_head = qb[:, h * HEAD : (h + 1) * HEAD]
        qs[h] = q_head
        qt[h] = q_head.T

    lane = lax.broadcasted_iota(jnp.int32, (1, rows), 1)
    q_doc = jnp.where(lane < BLK, doc[2 * i], doc[2 * i + 1])

    def bias(d):
        src = ctx_at(-d)
        return [jnp.where(q_doc == doc[2 * src + b], 0.0, NEG) for b in range(2)]

    def scores(k, place, d):
        k_blk = kv[place, 0]
        if d is None:
            key = lax.broadcasted_iota(jnp.int32, (rows, rows), 0)
            query = lax.broadcasted_iota(jnp.int32, (rows, rows), 1)
            k_doc = jnp.where(key < BLK, doc[2 * i], doc[2 * i + 1])
            allowed = (key <= query) & (k_doc == q_doc)
        else:
            b0, b1 = bias(d)
        for h in range(heads):
            s = dot(k_blk, qt[h])
            if d is None:
                s = jnp.where(allowed, s, NEG)
            sb[k, h] = s
            top = jnp.max(s.reshape(2, BLK // 8, 8, rows), axis=1) * c2
            if d is None:
                top = jnp.maximum(top[0], top[1])
            else:
                top = jnp.maximum(top[0] + b0, top[1] + b1)
            m8[h] = top if k == 0 else jnp.maximum(m8[h], top)

    def weigh(group, entries):
        tops = []
        alphas = []
        for h in range(heads):
            m = jnp.max(m8[h], axis=0, keepdims=True)
            if group > 0:
                m = jnp.maximum(m, mrun[h])
                alphas.append(jnp.exp2(mrun[h] - m))
            mrun[h] = m
            mg[group, h] = m
            tops.append(m)
        v_t = jnp.concatenate([kv[place, 1].T for place, _ in entries], axis=1)
        shifts = [None if d is None else bias(d) for _, d in entries]
        for h in range(heads):
            blocks = []
            total = None
            for k, (place, d) in enumerate(entries):
                s = sb[k, h] * c2
                if d is None:
                    p = jnp.exp2(s - tops[h])
                else:
                    b0, b1 = shifts[k]
                    p = jnp.concatenate(
                        [jnp.exp2(s[:BLK] - (tops[h] - b0)), jnp.exp2(s[BLK:] - (tops[h] - b1))],
                        axis=0,
                    )
                part_sum = jnp.sum(p.reshape(rows // 8, 8, rows), axis=0)
                total = part_sum if total is None else total + part_sum
                p = p.astype(BF16)
                pb[place, h] = p
                blocks.append(p)
            out = dot(v_t, jnp.concatenate(blocks, axis=0))
            if group > 0:
                total = total + l8[h] * alphas[h]
                out = out + acc[h] * alphas[h]
            l8[h] = total
            acc[h] = out

    with scope("slot0"):
        scores(0, 0, None)
    for c in range(chunks):
        cot_send(c, cross, c).start()
    with scope("grad0"):
        w_copy(t).wait()
        own_c.wait()
        gt[...] = dot_t(wb[t], cb[t])
    for b in range(2):
        with scope("wait8"):
            arrived(2, b)

        @pl.when(x >= 2)
        def _():
            near(2, 6, 3, b).start()

        if b == 0:
            with scope("grad1"):
                w_copy(partner).wait()
                cot_wait(partner, 0, chunks, 5)
                gt[...] += dot_t(wb[partner], cb[partner])

    with scope("score8"):
        scores(2, 2, 8)
    for b in range(2):
        with scope("wait4"):
            arrived(1, b)

        for e in (1, 3):

            @pl.when(x + e < GROUP)
            def _():
                near(1, 3 + e, e, b).start()

            @pl.when(x + e >= GROUP)
            def _():
                near(1, 2 + e, e, b).start()

    for b in range(2):

        @pl.when(x == 1)
        def _():
            near(2, 6, 3, b).start()

        @pl.when(x == GROUP - 1)
        def _():
            near(2, 4, 1, b).start()

    with scope("score4"):
        scores(1, 1, 4)

    up, down = 3 + last, 6 - first
    for b in range(2):
        with scope("waitup"):
            arrived(up, b)
        near(up, 7, 1, b).start()
    with scope("groupA"):
        weigh(0, [(0, None), (1, 4), (2, 8)])
    for b in range(2):
        with scope("waitdown"):
            arrived(down, b)
        near(down, 8, -1, b).start()
    rest_up, rest_down = 4 - last, 5 + first
    group_b = [
        (up, 1 + 4 * last),
        (down, 7 - 4 * first),
        (rest_up, 5 - 4 * last),
        (rest_down, 3 + 4 * first),
    ]
    for k, (place, d) in enumerate(group_b):
        if k >= 2:
            with scope("waitb"):
                arrived(place, 0)
        with scope("scoreb"):
            scores(k, place, d)
    with scope("groupB"):
        arrived(rest_up, 1)
        arrived(rest_down, 1)
        weigh(1, group_b)
    for c in range(3):
        with scope("cotx"):
            cot_wait(cross, c, c + 1, c)
        cot_pass(c).start()

    def grad_piece(s, lo, hi):
        cols = slice(lo * 256, hi * 256)
        gt[...] += dot_t(wb[s, :, cols], cb[s, :, cols])

    with scope("grad2"):
        w_copy(cross).wait()
        grad_piece(cross, 0, 3)
    group_c = [(7, 2), (8, 6)]
    for n, (place, d) in enumerate(group_c):
        with scope("waitc"):
            arrived(place, 0)
        scores(0, place, d)
        arrived(place, 1)
        with scope("groupC"):
            weigh(2 + n, [(place, d)])
    with scope("attn"):
        for h in range(heads):
            inv = 1.0 / jnp.sum(l8[h], axis=0, keepdims=True)
            linv[h] = inv
            a = (acc[h] * inv).astype(BF16)
            attn_t[h] = a
            attn[:, h * HEAD : (h + 1) * HEAD] = a.T

    def part(s, c):
        return dot(attn[...], wb[s, :, c * 256 : (c + 1) * 256])

    def to_partner(k, c):
        return send(pp.at[k, c], pr.at[k, c], ps, prs.at[chunks if k else c], i, partner)

    def to_cross(c):
        return send(xc.at[c], xr.at[c], xs, xrs, i, cross)

    with scope("diag"):
        w_copy(diag).wait()
        for c in range(chunks):
            pp[0, c] = part(diag, c).astype(BF16)
        for c in range(2):
            to_partner(0, c).start()
    for c in range(3, chunks):
        with scope("cotx"):
            cot_wait(cross, c, c + 1, c)
        cot_pass(c).start()
    for c in range(2, chunks):
        to_partner(0, c).start()

    def rs_step(lo, hi):
        with scope("rs1"):
            for c in range(lo, hi):
                to_partner(0, c).wait_recv()
                xc[c] = (po[c] + pr[0, c].astype(F32)).astype(BF16)
                to_cross(c).start()

    with scope("grad2"):
        grad_piece(cross, 3, chunks)
    with scope("cotd"):
        cot_wait(diag, 0, 3, 6)
    with scope("grad3"):
        grad_piece(diag, 0, 3)
    with scope("cross"):
        for c in range(chunks):
            po[c] = part(cross, c)
    rs_step(0, 2)
    with scope("cotd"):
        cot_wait(diag, 3, chunks, 7)
    with scope("grad3"):
        grad_piece(diag, 3, chunks)
    with scope("heads"):
        for h in range(heads):
            do_t = gt[h * HEAD : (h + 1) * HEAD].astype(BF16)
            dot_b[h] = do_t
            do_b[h] = do_t.T
            delta[h] = jnp.sum(do_t.astype(F32) * attn_t[h].astype(F32), axis=0, keepdims=True)

    def bwd_group(places, groups):
        weights = [[] for _ in places]
        grads = [[] for _ in places]
        for h in range(heads):
            for n, place in enumerate(places):
                f = jnp.exp2(mg[groups[n], h] - mrun[h]) * linv[h]
                p = pb[place, h].astype(F32) * f
                weights[n].append(p.astype(BF16))
                ds = (p * (dot(kv[place, 1], dot_b[h]) - delta[h])).astype(BF16)
                pb[place, h] = ds
                grads[n].append(ds)
        def values_part(n):
            w = jnp.concatenate(weights[n], axis=1)
            return dot(w, do_b[...].reshape(heads * rows, HEAD))

        def keys_part(n):
            ds = jnp.concatenate(grads[n], axis=1)
            return dot(ds, qs[...].reshape(heads * rows, HEAD)) * scale

        return keys_part, values_part

    def grad_relay(side, b):
        return send(
            gkv.at[7 + side, b],
            relay.at[side, b],
            gs,
            rr.at[side, b],
            peer(2 * side - 1),
            t,
        )

    def grad_near(side, j, b):
        return send(
            gkv.at[3 + 2 * side + j, b],
            rx.at[side, j, b],
            gs,
            gr.at[side, j, b],
            peer(2 * side - 1),
            t,
        )

    def bwd_step(k, carry):
        j_up = jnp.where(k == 1, 1 - last, last)
        j_down = jnp.where(k == 1, first, 1 - first)
        places = [jnp.where(k == 0, 7, 3 + j_up), jnp.where(k == 0, 8, 5 + j_down)]
        with scope("bwd"):
            parts = bwd_group(places, [jnp.where(k == 0, 2 + n, 1) for n in range(2)])
        for b in (1, 0):
            with scope("bwdpart"):
                done = [parts[b](n) for n in range(2)]

            @pl.when(k < 2)
            def _():
                for side, place in enumerate(places):
                    gkv[place, b] = done[side].astype(BF16)

            @pl.when(k == 2)
            def _():
                for side, place in enumerate(places):
                    with scope("waitrelay"):
                        grad_relay(side, b).wait_recv()
                    gkv[place, b] = (done[side] + relay[side, b].astype(F32)).astype(BF16)

            @pl.when(k == 0)
            def _():
                grad_relay(0, b).start()
                grad_relay(1, b).start()
                if b == 1:
                    rs_step(2, chunks)

            @pl.when(k > 0)
            def _():
                grad_near(0, j_up, b).start()
                grad_near(1, j_down, b).start()

        return carry

    lax.fori_loop(0, 3, bwd_step, 0)

    with scope("bwdown"):
        parts = bwd_group([0, 1, 2], [0] * 3)
        for n in range(3):
            for b in range(2):
                g3[n, b] = parts[b](n)

    with scope("partner"):
        for c in range(chunks):
            pp[1, c] = part(partner, c).astype(BF16)
        for c in range(chunks):
            to_partner(1, c).start()

    def grad_far(k, b):
        return send(
            gkv.at[k + 1, b], rz.at[k, b], gs, zr.at[k, b], ctx_at(-4 * k - 4), t
        )

    def near_sum(k, b):
        total = g3[k, b]
        for side, e in enumerate((1, 3)):
            j = k - lax.div(x + e, GROUP)
            block = rx[side, jnp.clip(j, 0, 1), b].astype(F32)
            total = total + jnp.where((j >= 0) & (j <= 1), block, 0.0)
        return total

    for b in (1, 0):
        with scope("gradnear"):
            for side in range(2):
                for j in range(2):
                    grad_near(side, j, b).wait_recv()
        with scope("nearsum"):
            for k in range(2):
                gkv[k + 1, b] = near_sum(k + 1, b).astype(BF16)
                grad_far(k, b).start()

    with scope("ownpart"):
        for c in range(chunks):
            po[c] = part(t, c)
    for b in range(2):
        g3[0, b] = near_sum(0, b)

    def put(n):
        src = (mixed, gq, gv, gk)[n]
        dst = (mixed_out, gq_out, gv_out, gk_out)[n]
        return pltpu.make_async_copy(src, dst, out_sem.at[n])

    with scope("dq"):
        for n in range(SLOTS):
            ktb[:, n * rows : (n + 1) * rows] = kv[n, 0].T
        for h in range(heads):
            dq_t = dot(ktb[...], pb[:, h].reshape(SLOTS * rows, rows))
            gq[:, h * HEAD : (h + 1) * HEAD] = (dq_t * scale).T.astype(BF16)
    put(1).start()
    with scope("rscross"):
        send(pp.at[1], pr.at[1], ps, prs.at[chunks], i, partner).wait_recv()
        send(xc, xr, xs, xrs, i, cross).wait_recv()
    for c in range(chunks):
        mixed[:, c * 256 : (c + 1) * 256] = (
            po[c] + pr[1, c].astype(F32) + xr[c].astype(F32)
        ).astype(BF16)
    put(0).start()
    with scope("sent"):
        block = kv.at[pl.ds(1, SLOTS - 1)]
        send(block, block, ks, kr.at[0, 0], i, partner).wait_send()
        block = cb.at[pl.ds(0, 3)]
        send(block, block, cs, cr.at[0], i, partner).wait_send()
        send(pp, pr, ps, prs.at[0], i, partner).wait_send()
        send(xc, xr, xs, xrs, i, cross).wait_send()
    for b, result in ((1, gv), (0, gk)):
        for k in range(2):
            with scope("gradfar"):
                grad_far(k, b).wait_recv()
        result[...] = (g3[0, b] + rz[0, b].astype(F32) + rz[1, b].astype(F32)).astype(BF16)
        put(3 - b).start()

    with scope("put"):
        for n in range(4):
            put(n).wait()
        block = gkv.at[pl.ds(1, SLOTS - 1)]
        send(block, block, gs, zr.at[0, 0], i, partner).wait_send()


def leave(*refs):
    count = (len(refs) - 1) // 2
    sem = refs[-1]
    copies = [
        pltpu.make_async_copy(refs[n], refs[count + n], sem.at[n]) for n in range(count)
    ]
    for copy in copies:
        copy.start()
    for copy in copies:
        copy.wait()


def on_device(queries, keys, values, out_weight, cotangent, doc_ids):
    n_ctx = lax.axis_size("ctx")
    rows = queries.shape[0]
    heads = queries.shape[1] // HEAD
    chunks = cotangent.shape[1] // 256
    any_space = pl.BlockSpec(memory_space=pl.ANY)
    hbm = pl.BlockSpec(memory_space=pltpu.HBM)
    dma = pltpu.SemaphoreType.DMA
    shapes = tuple(
        jax.ShapeDtypeStruct(like.shape, BF16) for like in (cotangent, queries, keys, values)
    )
    results = pl.pallas_call(
        functools.partial(kernel, n_ctx, heads, rows, chunks),
        out_shape=shapes,
        in_specs=[hbm] * 6,
        out_specs=(any_space,) * 4,
        scratch_shapes=[
            *[pltpu.VMEM(shape.shape, BF16) for shape in shapes],
            dma((4,)),
            pltpu.SMEM(doc_ids.shape, jnp.int32),
            pltpu.VMEM((rows, heads * HEAD), BF16),
            pltpu.VMEM((heads, rows, HEAD), BF16),
            pltpu.VMEM((SLOTS, 2, rows, HEAD), BF16),
            pltpu.VMEM((4, heads * HEAD, chunks * 256), BF16),
            pltpu.VMEM((4, rows, chunks * 256), BF16),
            pltpu.VMEM((heads, HEAD, rows), BF16),
            pltpu.VMEM((4, heads, rows, rows), F32),
            pltpu.VMEM((SLOTS, heads, rows, rows), BF16),
            pltpu.VMEM((4, heads, 1, rows), F32),
            pltpu.VMEM((heads, 8, rows), F32),
            pltpu.VMEM((heads, 1, rows), F32),
            pltpu.VMEM((heads, 8, rows), F32),
            pltpu.VMEM((heads, 1, rows), F32),
            pltpu.VMEM((heads, HEAD, rows), F32),
            pltpu.VMEM((heads, HEAD, rows), BF16),
            pltpu.VMEM((rows, heads * HEAD), BF16),
            pltpu.VMEM((heads * HEAD, rows), F32),
            pltpu.VMEM((heads, HEAD, rows), BF16),
            pltpu.VMEM((heads, rows, HEAD), BF16),
            pltpu.VMEM((heads, 1, rows), F32),
            pltpu.VMEM((HEAD, SLOTS * rows), BF16),
            pltpu.VMEM((SLOTS, 2, rows, HEAD), BF16),
            pltpu.VMEM((3, 2, rows, HEAD), F32),
            pltpu.VMEM((2, 2, rows, HEAD), BF16),
            pltpu.VMEM((2, 2, 2, rows, HEAD), BF16),
            pltpu.VMEM((2, 2, rows, HEAD), BF16),
            pltpu.VMEM((2, chunks, rows, 256), BF16),
            pltpu.VMEM((2, chunks, rows, 256), BF16),
            pltpu.VMEM((chunks, rows, 256), BF16),
            pltpu.VMEM((chunks, rows, 256), BF16),
            pltpu.VMEM((chunks, rows, 256), F32),
            dma,
            dma,
            dma((2,)),
            dma((4,)),
            dma,
            dma,
            dma((SLOTS, 2)),
            dma,
            dma((8,)),
            dma((2, 2)),
            dma,
            dma((2, 2, 2)),
            dma((2, 2)),
            dma,
            dma((chunks + 1,)),
            dma,
            dma,
        ],
        compiler_params=pltpu.CompilerParams(
            collective_id=0, has_side_effects=True, vmem_limit_bytes=50 * 1024 * 1024
        ),
    )(
        *[
            pltpu.with_memory_space_constraint(a, pltpu.HBM)
            for a in (doc_ids, queries, keys, values, out_weight, cotangent)
        ]
    )
    return pl.pallas_call(
        leave,
        out_shape=shapes,
        in_specs=[any_space] * 4,
        out_specs=(any_space,) * 4,
        scratch_shapes=[dma((4,))],
        compiler_params=pltpu.CompilerParams(vmem_limit_bytes=1024 * 1024),
    )(*results)


def solution(mesh):
    return jax.shard_map(
        on_device,
        mesh=mesh,
        in_specs=(
            P("ctx", "tp"),
            P("ctx", "tp"),
            P("ctx", "tp"),
            P("tp", None),
            P("ctx", "tp"),
            P(),
        ),
        out_specs=(P("ctx", "tp"), P("ctx", "tp"), P("ctx", "tp"), P("ctx", "tp")),
        check_vma=False,
    )
```
